32 devices in a mesh: gx: 8 (over z, y), gy: 4 (over x, core).
Axes of the slice: x: 2, y: 2, z: 4, core: 2. Of those that a mesh axis runs over, the one named last changes fastest.
Arguments:
- charges: float32 [256, 128, 256], P('gx', 'gy'), may hold values from -6 to 6
- kernel_taps: float32 [3, 3, 21], replicated, may hold values from -1.08 to 1.08
Outputs:
- potential: float32 [256, 128, 256], P('gx', 'gy')
The draws below stay inside these ranges and needn't reach their ends.
All inputs are finite; a program needn't handle non-finite values.
Results may differ from the reference program's by a relative error of at most 0.035.
Values sent between devices are 32-bit elements; how exact they have to be, the bound alone decides.
A program may use at most 128 MiB of HBM per device.

```python
import jax
import jax.numpy as jnp
from jax import lax

NZ = 256
TERMS = 3
LEVELS = 3
NX = 256
NY = 128
TAPS = 21


def shard_levels(key, shape, pieces, least, high):
    factor_of = 1.0
    for position, shards_of in pieces:
        heights = jax.random.uniform(jax.random.fold_in(jax.random.fold_in(key, 6), position), (shards_of,), jnp.float32, least / len(pieces), high / len(pieces))
        factor_of = factor_of * jnp.repeat(jnp.exp(heights), shape[position] // shards_of).reshape((-1,) + (1,) * (len(shape) - 1 - position))
    return factor_of


def bell_draw(key, dims, scale, bound, cuts=(), held_as=jnp.bfloat16):
    values = scale * jax.random.normal(key, dims, jnp.float32)
    if cuts:
        values = values * shard_levels(key, dims, cuts, -0.22, 0.18)
    return jnp.clip(values, -bound, bound).astype(held_as)


def setup_inputs(seed: int = 0) -> dict:
    key_of = jax.random.split(jax.random.key(seed), 3)
    charges = bell_draw(key_of[0], (NX, NY, NZ), 1.0, 6.0, ((0, 8), (1, 4)), jnp.float32)
    kernel_taps = bell_draw(key_of[1], (LEVELS, TERMS, TAPS), 0.18, 1.08, (), jnp.float32)
    return dict(charges=charges, kernel_taps=kernel_taps)


SPLINE = (0.125, 0.5, 0.75, 0.5, 0.125)


def correlate(values, taps, along):
    length = values.shape[along]
    tap_count = taps.shape[0]
    radius = tap_count // 2
    wrapped = (jnp.arange(tap_count, dtype=jnp.int32) - radius) % length
    onehot = (wrapped[:, None] == jnp.arange(length, dtype=jnp.int32)[None, :]).astype(jnp.float32)
    profile = jnp.dot(taps, onehot, preferred_element_type=jnp.float32, precision=lax.Precision.HIGHEST)
    shaped = [1] * values.ndim
    shaped[along] = -1
    spectrum = jnp.fft.rfft(values, axis=along) * jnp.conj(jnp.fft.rfft(profile)).reshape(shaped)
    return jnp.fft.irfft(spectrum, n=length, axis=along)


def convolve(values, taps):
    summed = jnp.zeros(values.shape, jnp.float32)
    for member in range(taps.shape[0]):
        sectioned = correlate(values, taps[member], 0)
        sectioned = correlate(sectioned, taps[member], 1)
        summed = summed + correlate(sectioned, taps[member], 2)
    return summed


def restrict(values, along):
    length = values.shape[along]
    summed = jnp.zeros(values.shape, jnp.float32)
    for shift_by in range(-2, 3):
        summed = summed + SPLINE[shift_by + 2] * jnp.roll(values, -shift_by, along)
    return lax.slice_in_dim(summed, 0, length, 2, along)


def prolong(values, along):
    blank = jnp.zeros(values.shape, jnp.float32)
    shaped = list(values.shape)
    shaped[along] = 2 * shaped[along]
    spread = jnp.stack([values, blank], axis=along + 1).reshape(shaped)
    summed = jnp.zeros(spread.shape, jnp.float32)
    for shift_by in range(-2, 3):
        summed = summed + SPLINE[shift_by + 2] * jnp.roll(spread, shift_by, along)
    return summed


def restrict_grid(values):
    return restrict(restrict(restrict(values, 0), 1), 2)


def prolong_grid(values):
    return prolong(prolong(prolong(values, 0), 1), 2)


def reference(charges, kernel_taps):
    coarse = restrict_grid(charges)
    summit = restrict_grid(coarse)
    top_field = convolve(summit, kernel_taps[2])
    middle = convolve(coarse, kernel_taps[1]) + prolong_grid(top_field)
    return convolve(charges, kernel_taps[0]) + prolong_grid(middle)
```

```python
import functools

import jax
import jax.numpy as jnp
import numpy as np
from jax import lax
from jax.experimental import pallas as pl
from jax.experimental.pallas import tpu as pltpu
from jax.sharding import PartitionSpec as P

SPLINE = (0.125, 0.5, 0.75, 0.5, 0.125)
F32, BF16 = jnp.float32, jnp.bfloat16
MESH = pl.DeviceIdType.MESH


def spline_at(offset):
    return SPLINE[offset + 2] if -2 <= offset <= 2 else 0.0


def fixed_table(rows, cols, width):
    table = np.zeros((width, len(cols)), np.float32)
    for a, fine in enumerate(rows):
        for b, other in enumerate(cols):
            if fine is not None and other is not None:
                table[a, b] = spline_at(other - 2 * fine)
    return table


def lifted_table(rows, cols, width):
    table = np.zeros((width, len(cols)), np.float32)
    for a, fine in enumerate(rows):
        for b, coarse in enumerate(cols):
            if coarse is not None:
                table[a, b] = spline_at(fine - 2 * coarse)
    return table


def twice(table):
    return jnp.asarray(np.concatenate([table, table], axis=1), BF16)


def halves(value):
    high = value.astype(BF16)
    return high, (value - high.astype(F32)).astype(BF16)


def dot(left, right):
    return jnp.dot(left, right, preferred_element_type=F32)


def stacked2(value):
    high, low = halves(value)
    return jnp.concatenate([high, low], axis=0)


def stacked3(value):
    high, low = halves(value)
    return jnp.concatenate([high, low, high], axis=0)


def repeat(count, step, body):
    def trip(i, carry):
        for k in range(step):
            body(i * step + k)
        return carry

    assert count % step == 0
    lax.fori_loop(0, count // step, trip, 0)


def kernel(nx, ny, radius, terms, taps, q, ry1, rz1, ry2, rz2, uy2, uz2, uy1, uz1, out,
           fine, mid, ext, got, left1, right1, low1, high1, l2p, cols2, seen2, top,
           ty0, ty1, ty2, tz0, tz1, tz2, y0, s0, y1, s1, y2, s2, r1, l1w, l2y, tx, ty, md, my,
           send, recv):
    bx, by, bz = q.shape
    hx, hy, hz = bx // 2, by // 2, bz // 2
    ex, ey, ez = bx // 4, by // 4, bz // 4
    count = 2 * radius + 1
    margin = radius + 1
    me_x, me_y = lax.axis_index("gx"), lax.axis_index("gy")
    reach = 2
    odd = lax.rem(me_x, 2) if nx % 2 == 0 else 0
    even = 1 - odd
    wy = min(ny, 2 * reach + 1)
    low_y = -((wy - 1) // 2)

    def device(dx, dy):
        return {"gx": lax.rem(me_x + dx + nx, nx), "gy": lax.rem(me_y + dy + ny, ny)}

    peers = {}
    for dx, dy in [(-1, 0), (1, 0), (0, -1), (0, 1), (-2, 0), (2, 0)] + [
        (0, -(low_y + k)) for k in range(wy)
    ]:
        if dx % nx or dy % ny:
            peers[(dx % nx, dy % ny)] = (dx, dy)
    barrier = pltpu.get_barrier_semaphore()
    for dx, dy in peers.values():
        pl.semaphore_signal(barrier, inc=1, device_id=device(dx, dy), device_id_type=MESH)

    def tap(level, member, position):
        return taps[level, member, position]

    def band(level, member, rows, cols, first, cycle, places):
        column = lax.broadcasted_iota(jnp.int32, (rows, cols), 1)
        place = column
        for start, shift in places:
            place = jnp.where(column >= start, column + shift, place)
        offsets = place - lax.broadcasted_iota(jnp.int32, (rows, cols), 0) + first
        if cycle:
            offsets = jnp.where(offsets < 0, offsets + cycle, offsets)
            offsets = jnp.where(offsets >= cycle, offsets - cycle, offsets)
        table = jnp.zeros((rows, cols), F32)
        for position in range(count):
            table = jnp.where(offsets == position, tap(level, member, position), table)
        return table

    def y_table(ref, level, rows, cols, first, cycle, places):
        for member in range(terms):
            high, low = halves(band(level, member, rows, cols, first, cycle, places))
            at = slice(member * rows, (member + 1) * rows)
            ref[at, 0:cols] = high
            ref[at, cols : 2 * cols] = high
            ref[at, 2 * cols : 3 * cols] = low

    def z_table(ref, level, n):
        def rows_of(i):
            start = pl.multiple_of(i * 16, 16)
            offsets = (
                lax.broadcasted_iota(jnp.int32, (16, n), 0)
                + start
                - lax.broadcasted_iota(jnp.int32, (16, n), 1)
                + radius
            )
            offsets = jnp.where(offsets < 0, offsets + n, offsets)
            offsets = jnp.where(offsets >= n, offsets - n, offsets)
            for member in range(terms):
                table = jnp.zeros((16, n), F32)
                for position in range(count):
                    table = jnp.where(offsets == position, tap(level, member, position), table)
                high, low = halves(table)
                ref[0, pl.ds(pl.multiple_of(member * n + start, 16), 16), :] = high
                ref[1, pl.ds(pl.multiple_of(member * n + start, 16), 16), :] = low

        repeat(n // 16, 1, rows_of)

    sem = [0]

    def remote(source, target, dx, dy):
        index = sem[0]
        sem[0] += 1
        return pltpu.make_async_remote_copy(
            src_ref=source, dst_ref=target, send_sem=send.at[index], recv_sem=recv.at[index],
            device_id=device(dx, dy), device_id_type=MESH,
        )

    def both(copies):
        for copy in copies:
            copy.start()
        return copies

    def arrive(copies):
        for copy in copies:
            copy.wait_recv()

    x0, x1 = radius, radius + bx
    extra = radius - 8
    per = 8 // extra
    def weighted(source, i, low, high):
        total = None
        for k in range(-2, 3):
            if low <= 2 * i + k < high:
                piece = source(2 * i + k) * SPLINE[k + 2]
                total = piece if total is None else total + piece
        return total

    rows1, rows2 = hx + 2, ex + 3
    half2 = l2p.shape[0]
    wide1, wide2 = ry1.shape[0], ry2.shape[0]
    for i in range(rows1):
        r1[i] = dot(ry1[...], stacked2(weighted(lambda f: q[f], i - 1, 0, bx)))
    high, low = halves(r1[...].reshape(rows1 * wide1, bz))
    l1w[...] = (dot(high, rz1[...]) + dot(low, rz1[...])).reshape(rows1, wide1, hz)
    for i in range(rows2):
        l2y[i] = dot(ry2[...], stacked2(weighted(lambda f: l1w[f + 1], i - 1, -1, hx + 1)))
    for i in range(rows2, 2 * half2):
        l2y[i] = jnp.zeros((wide2, hz), F32)
    high, low = halves(jnp.concatenate([l2y[0:half2], l2y[half2 : 2 * half2]], axis=2).reshape(half2 * wide2, 2 * hz))
    l2p[...] = (dot(high, rz2[...]) + dot(low, rz2[...])).reshape(l2p.shape)
    pl.semaphore_wait(barrier, len(peers))
    spot = -low_y
    lines = both([
        remote(l2p, seen2.at[0], 1, 0),
        remote(l2p, seen2.at[1], -1, 0),
        remote(l2p, seen2.at[2], 2, 0),
        remote(l2p, seen2.at[3], -2, 0),
    ])
    rim = both([
        remote(l1w.at[rows1 - margin - 1 : rows1], low1, 1, 0),
        remote(l1w.at[0 : margin + 1], high1, -1, 0),
    ])
    g1 = bx // per
    steps = near_steps(radius)
    side = both([
        remote(q.at[:, by - 8 : by], fine.at[x0:x1, by : by + 8], 0, 1),
        remote(q.at[:, 0:8], fine.at[x0:x1, by + 8 : by + 16], 0, -1),
    ])
    for i in range(bx):
        g, r = i // per, extra * (i % per)
        ext[0, g, r : r + extra] = q[i, by - radius : by - 8]
        ext[1, g, r : r + extra] = q[i, 8:radius]

    side += both([
        remote(ext.at[0, 0:g1], got.at[0, 0:g1], 0, 1),
        remote(ext.at[1, 0:g1], got.at[1, 0:g1], 0, -1),
    ])
    def pick(first, second):
        return even * first + odd * second

    def span(start, size):
        return pl.ds(start, size)

    near = [
        both([remote(q.at[span(pick(bx - b, a), b - a)], fine.at[span(pick(x0 - b, x1 + a), b - a), 0:by], even - odd, 0)])
        for a, b in steps
    ]
    places2 = []
    for k in range(wy):
        at = wide2 * k
        places2 += [(at, ey * k - at), (at + ey + 2, ey * k - 3 - ey - at), (at + ey + 3, 1000)]
    y_table(ty2, 2, wide2, wy * wide2, low_y * ey + 1 + radius, wy * ey if ny <= 2 * reach + 1 else 0, places2)
    z_table(tz2, 2, ez)
    fine[x0:x1, 0:by, :] = q[...]
    y_table(ty0, 0, by, by + 24, radius, 0, [(by, -by - 8), (by + 8, -8), (by + 16, -by - 16 - radius), (by + 16 + extra, -8 - extra), (by + 16 + 2 * extra, 1000)])
    y_table(ty1, 1, wide1, wide1 + 2 * hy, radius + 1, 0, [(hy + 1, -hy - 2), (hy + 2, 1000), (wide1, -wide1 - hy + 1), (wide1 + hy, -wide1 - 1)])
    z_table(tz0, 0, bz)
    spare = jnp.zeros((8 - 2 * extra, bz), F32)

    def unpack(rows, first):
        for n, i in enumerate(rows):
            g, r = first + n // per, extra * (n % per)
            fine[i, by + 16 : by + 16 + extra] = got[0, g, r : r + extra]
            fine[i, by + 16 + extra : by + 16 + 2 * extra] = got[1, g, r : r + extra]
            fine[i, by + 16 + 2 * extra : by + 24] = spare

    z_table(tz1, 1, hz)

    arrive(lines)
    home = radius
    pairs = cols2.shape[1]
    whole = [None] * (2 * pairs)
    for first, source in ((home, l2p), (home - ex, seen2.at[0]), (home + ex, seen2.at[1]), (home - 2 * ex, seen2.at[2]), (home + 2 * ex, seen2.at[3])):
        for r in range(rows2):
            if 0 <= first + r < rows2 + 2 * radius:
                piece = source[r % half2][:, (r // half2) * ez : (r // half2 + 1) * ez]
                whole[first + r] = piece if whole[first + r] is None else whole[first + r] + piece
    for j in range(pairs):
        top[j] = jnp.concatenate([jnp.zeros((wide2, ez), F32) if v is None else v for v in (whole[j], whole[j + pairs])], axis=1)
    fan = both([remote(top, cols2.at[k], 0, -(low_y + k)) for k in range(wy) if low_y + k])
    cols2[-low_y] = top[...]
    arrive(rim)
    mid[0 : margin + 1, 0:wide1] = low1[...]
    mid[margin + 1 : margin + hx - 1, 0:wide1] = l1w[2:hx]
    mid[margin + hx - 1 : margin + hx + margin, 0:wide1] = high1[...]
    for i, j in ((margin - 1, 0), (margin, 1), (margin + hx - 1, hx), (margin + hx, hx + 1)):
        mid[i, 0:wide1] += l1w[j]
    left1[...] = mid[:, 1 : hy + 1, :]
    right1[:, 0:1, :] = mid[:, hy + 1 : hy + 2, :]
    right1[:, 1:hy, :] = mid[:, 0 : hy - 1, :]
    rim2 = both([
        remote(left1, mid.at[:, wide1 : wide1 + hy], 0, 1),
        remote(right1, mid.at[:, wide1 + hy : wide1 + 2 * hy], 0, -1),
    ])
    far = both([remote(q.at[span(pick(0, bx - radius), radius)], fine.at[span(pick(x1, 0), radius), 0:by], odd - even, 0)])

    def correlate_y(ref, source, table, rows, step, first=0):
        width = table.shape[0] // terms

        def one(i):
            i = i + first
            value = dot(table[...], stacked3(source[i]))
            for member in range(terms):
                ref[member, i] = value[member * width : (member + 1) * width]

        repeat(rows, step, one)

    def correlate_x(ref, source, level, rows, first, step, start=0):
        def one(i):
            i = i + start
            for member in range(terms):
                total = None
                for position in range(count):
                    piece = source[member, i + first + position] * tap(level, member, position)
                    total = piece if total is None else total + piece
                high, low = halves(total)
                at = slice(member * total.shape[1], (member + 1) * total.shape[1])
                ref[0, i, :, at] = high
                ref[1, i, :, at] = low

        repeat(rows, step, one)

    def correlate_z(ref, table, rows, count):
        size = count * ref.shape[2]
        high = ref[0, rows].reshape(size, ref.shape[3])
        low = ref[1, rows].reshape(size, ref.shape[3])
        return dot(high, table[0]) + dot(low, table[0]) + dot(high, table[1])

    def prolong_x(source, j, first):
        at = j - 2 * first
        if j % 2 == 0:
            c = (j // 2) - first
            return source[c - 1] * 0.125 + source[c] * 0.75 + source[c + 1] * 0.125
        c = (j - 1) // 2 - first
        return source[c] * 0.5 + source[c + 1] * 0.5

    arrive(side)
    unpack(range(x0, x1), 0)
    correlate_y(y0, fine, ty0, bx, 4, x0)
    correlate_x(s0, y0, 0, bx - 2 * radius, 0, 1, radius)
    def pack(start, size, group):
        for n in range(size):
            g, r = group + n // per, extra * (n % per)
            ext[0, g, r : r + extra] = fine[start + n, by - radius : by - 8, :]
            ext[1, g, r : r + extra] = fine[start + n, 8:radius, :]
        rows, groups = span(start, size), slice(group, group - (-size // per))
        return both([
            remote(fine.at[rows, by - 8 : by], fine.at[rows, by : by + 8], 0, 1),
            remote(fine.at[rows, 0:8], fine.at[rows, by + 8 : by + 16], 0, -1),
            remote(ext.at[0, groups], got.at[0, groups], 0, 1),
            remote(ext.at[1, groups], got.at[1, groups], 0, -1),
        ])

    parts = [(0, radius, pick(0, x1), pick(0, bx - radius))] + [
        (a, b, pick(x1 + a, x0 - b), pick(bx - radius + a, radius - b)) for a, b in steps
    ]
    groups = [g1]
    for a, b, _, _ in parts:
        groups.append(groups[-1] + -(-(b - a) // per))
    corners = []

    def relay(copies):
        part = len(corners)
        a, b, halo, _ = parts[part]
        arrive(copies)
        corners.append(pack(halo, b - a, groups[part]))

    arrive(fan)
    for j in range(pairs):
        value = dot(ty2[...], stacked3(jnp.concatenate([cols2[k, j] for k in range(wy)], axis=0)))
        for member in range(terms):
            y2[member, j] = value[member * wide2 : (member + 1) * wide2, 0:ez]
            y2[member, j + pairs] = value[member * wide2 : (member + 1) * wide2, ez : 2 * ez]
    correlate_x(s2, y2, 2, rows2, 0, 1)
    tx[...] = correlate_z(s2, tz2, slice(0, rows2), rows2).reshape(tx.shape)
    for j in range(hx + 2):
        ty[j] = dot(uy2[...], stacked2(prolong_x(tx, j - 1, -1)))
    high, low = halves(ty[...].reshape((hx + 2) * ty.shape[1], ez))
    lifted = dot(high, uz2[...]) + dot(low, uz2[...])

    md[...] = lifted.reshape(md.shape)
    relay(far)
    arrive(rim2)
    correlate_y(y1, mid, ty1, hx + 2 * margin, (hx + 2 * margin) // 2)
    correlate_x(s1, y1, 1, hx + 2, 0, 1)
    md[...] += correlate_z(s1, tz1, slice(0, hx + 2), hx + 2).reshape(md.shape)
    for j in range(bx):
        high, low = halves(dot(uy1[...], stacked2(prolong_x(md, j, -1))))
        my[0, j] = high
        my[1, j] = low

    def finish(start, size):
        rows = span(start, size)
        high = my[0, rows].reshape(size * by, hz)
        low = my[1, rows].reshape(size * by, hz)
        total = correlate_z(s0, tz0, rows, size) + dot(high, uz1[...]) + dot(low, uz1[...])
        out[rows] = total.reshape(size, by, bz)

    for copies in near:
        relay(copies)
    finish(radius, bx - 2 * radius)
    for part, (a, b, halo, target) in enumerate(parts):
        arrive(corners[part])
        unpack([halo + n for n in range(b - a)], groups[part])
        correlate_y(y0, fine, ty0, b - a, 2, halo)
        correlate_x(s0, y0, 0, b - a, 0, 1, target)
        finish(target, b - a)
    for copy in fan + rim + side + lines + sum(near, []) + far + rim2 + sum(corners, []):
        copy.wait_send()


def near_steps(radius):
    first = min(radius, radius // 2 + radius // 2 % 2)
    return [(0, first), (first, radius)]


def cyclic_restrict(n):
    rows = np.arange(n)[:, None]
    cols = np.arange(n // 2)[None, :]
    table = np.zeros((n, n // 2), np.float32)
    for k in range(-2, 3):
        table += SPLINE[k + 2] * ((2 * cols + k) % n == rows)
    return table


def body(charges, kernel_taps):
    nx, ny = lax.axis_size("gx"), lax.axis_size("gy")
    levels, terms, count = kernel_taps.shape
    radius = count // 2
    margin = radius + 1
    bx, by, bz = charges.shape
    hx, hy, hz = bx // 2, by // 2, bz // 2
    ex, ey, ez = bx // 4, by // 4, bz // 4
    pad = 16
    wy = min(ny, 5)
    order1 = list(range(hy)) + [hy, -1] + [None] * 6
    ry1 = fixed_table(order1, list(range(by)), len(order1))
    order2 = list(range(ey)) + [ey, ey + 1, -1] + [None] * 5
    ry2 = fixed_table(order2, order1, len(order2))
    rz1, rz2 = cyclic_restrict(bz), cyclic_restrict(hz)
    wide1 = hy + 8
    wide2 = ey + 8
    uy2 = lifted_table(list(range(-1, hy + 1)), list(range(-1, ey + 2)) + [None] * (wide2 - ey - 3), wide1)
    uy1 = lifted_table(list(range(by)), list(range(-1, hy + 1)) + [None] * (wide1 - hy - 2), by)
    fixed = [twice(ry1), jnp.asarray(rz1, BF16), twice(ry2), jnp.asarray(np.kron(np.eye(2), rz2), BF16), twice(uy2),
             jnp.asarray(rz2.T, BF16), twice(uy1), jnp.asarray(rz1.T, BF16)]
    rows1, rows2 = hx + 2, ex + 3
    half2, pairs = (rows2 + 1) // 2, (rows2 + 2 * radius + 1) // 2
    extra = radius - 8
    packed = bx * extra // 8 + sum(-(-(b - a) * extra // 8) for a, b in near_steps(radius) + [(0, radius)])
    scratch = [
        pltpu.VMEM(shape, dtype)
        for shape, dtype in (
            ((bx + 2 * radius, by + 24, bz), F32),
            ((hx + 2 * margin, wide1 + 2 * hy, hz), F32),
            ((2, packed, 8, bz), F32),
            ((2, packed, 8, bz), F32),
            ((hx + 2 * margin, hy, hz), F32),
            ((hx + 2 * margin, hy, hz), F32),
            ((margin + 1, wide1, hz), F32),
            ((margin + 1, wide1, hz), F32),
            ((half2, wide2, 2 * ez), F32),
            ((wy, pairs, wide2, 2 * ez), F32),
            ((4, half2, wide2, 2 * ez), F32),
            ((pairs, wide2, 2 * ez), F32),
            ((terms * by, 3 * (by + 24)), BF16),
            ((terms * wide1, 3 * (wide1 + 2 * hy)), BF16),
            ((terms * wide2, 3 * wy * wide2), BF16),
            ((2, terms * bz, bz), BF16),
            ((2, terms * hz, hz), BF16),
            ((2, terms * ez, ez), BF16),
            ((terms, bx + 2 * radius, by, bz), F32),
            ((2, bx, by, terms * bz), BF16),
            ((terms, hx + 2 * margin, wide1, hz), F32),
            ((2, hx + 2, wide1, terms * hz), BF16),
            ((terms, 2 * pairs, wide2, ez), F32),
            ((2, rows2, wide2, terms * ez), BF16),
            ((rows1, wide1, bz), F32),
            ((rows1, wide1, hz), F32),
            ((2 * half2, wide2, hz), F32),
            ((rows2, wide2, ez), F32),
            ((hx + 2, wide1, ez), F32),
            ((hx + 2, wide1, hz), F32),
            ((2, bx, by, hz), BF16),
        )
    ] + [
        pltpu.SemaphoreType.DMA((48,)),
        pltpu.SemaphoreType.DMA((48,)),
    ]
    return pl.pallas_call(
        functools.partial(kernel, nx, ny, radius, terms),
        out_shape=jax.ShapeDtypeStruct(charges.shape, F32),
        in_specs=[pl.BlockSpec(memory_space=pltpu.SMEM)] + [pl.BlockSpec(memory_space=pltpu.VMEM)] * 9,
        out_specs=pl.BlockSpec(memory_space=pltpu.VMEM),
        scratch_shapes=scratch,
        compiler_params=pltpu.CompilerParams(
            collective_id=0, has_side_effects=True, vmem_limit_bytes=60 * 2**20
        ),
    )(kernel_taps, charges, *fixed)


def solution(mesh):
    return jax.shard_map(
        body,
        mesh=mesh,
        in_specs=(P("gx", "gy", None), P()),
        out_specs=P("gx", "gy", None),
        check_vma=False,
    )
```

```python
import functools

import jax
import jax.numpy as jnp
import numpy as np
from jax import lax
from jax.experimental import pallas as pl
from jax.experimental.pallas import tpu as pltpu
from jax.sharding import PartitionSpec as P

SPLINE = (0.125, 0.5, 0.75, 0.5, 0.125)
F32, BF16 = jnp.float32, jnp.bfloat16
MESH = pl.DeviceIdType.MESH


def spline_at(offset):
    return SPLINE[offset + 2] if -2 <= offset <= 2 else 0.0


def fixed_table(rows, cols, width):
    table = np.zeros((width, len(cols)), np.float32)
    for a, fine in enumerate(rows):
        for b, other in enumerate(cols):
            if fine is not None and other is not None:
                table[a, b] = spline_at(other - 2 * fine)
    return table


def lifted_table(rows, cols, width):
    table = np.zeros((width, len(cols)), np.float32)
    for a, fine in enumerate(rows):
        for b, coarse in enumerate(cols):
            if coarse is not None:
                table[a, b] = spline_at(fine - 2 * coarse)
    return table


def twice(table):
    return jnp.asarray(np.concatenate([table, table], axis=1), BF16)


def halves(value):
    high = value.astype(BF16)
    return high, (value - high.astype(F32)).astype(BF16)


def dot(left, right):
    return jnp.dot(left, right, preferred_element_type=F32)


def stacked2(value):
    high, low = halves(value)
    return jnp.concatenate([high, low], axis=0)


def stacked3(value):
    high, low = halves(value)
    return jnp.concatenate([high, low, high], axis=0)


def repeat(count, step, body):
    def trip(i, carry):
        for k in range(step):
            body(i * step + k)
        return carry

    assert count % step == 0
    lax.fori_loop(0, count // step, trip, 0)


def kernel(nx, ny, radius, terms, *refs):
    given, out, held, refs = refs[:10], refs[10], refs[11:20], refs[20:]
    taps, ry1, rz1, ry2, rz2, uy2, uz2, uy1, uz1 = held
    (fine, mid, ext, got, left1, right1, low1, high1, l2p, cols2, seen2, top,
           ty0, ty1, ty2, tz0, tz1, tz2, y0, s0, y1, s1, y2, s2, r1, l1w, l2y, tx, ty, md, my,
     edge, edge_in, stage, send, recv, load, store) = refs
    bx, by, bz = given[1].shape
    x0, x1 = radius, radius + bx
    hx, hy, hz = bx // 2, by // 2, bz // 2
    ex, ey, ez = bx // 4, by // 4, bz // 4
    count = 2 * radius + 1
    margin = radius + 1
    me_x, me_y = lax.axis_index("gx"), lax.axis_index("gy")
    reach = 2
    odd = lax.rem(me_x, 2) if nx % 2 == 0 else 0
    even = 1 - odd
    wy = min(ny, 2 * reach + 1)
    low_y = -((wy - 1) // 2)

    def device(dx, dy):
        return {"gx": lax.rem(me_x + dx + nx, nx), "gy": lax.rem(me_y + dy + ny, ny)}

    peers = {}
    for dx, dy in [(-1, 0), (1, 0), (0, -1), (0, 1), (-2, 0), (2, 0)] + [
        (0, -(low_y + k)) for k in range(wy)
    ]:
        if dx % nx or dy % ny:
            peers[(dx % nx, dy % ny)] = (dx, dy)
    barrier = pltpu.get_barrier_semaphore()
    for dx, dy in peers.values():
        pl.semaphore_signal(barrier, inc=1, device_id=device(dx, dy), device_id_type=MESH)

    fetched = [
        pltpu.make_async_copy(source, target, load.at[n])
        for n, (source, target) in enumerate(zip(given, [taps, fine.at[x0:x1, 0:by]] + list(held[1:])))
    ]
    for copy in fetched:
        copy.start()

    def tap(level, member, position):
        return taps[level, member, position]

    def band(level, member, rows, cols, first, cycle, places):
        column = lax.broadcasted_iota(jnp.int32, (rows, cols), 1)
        place = column
        for start, shift in places:
            place = jnp.where(column >= start, column + shift, place)
        offsets = place - lax.broadcasted_iota(jnp.int32, (rows, cols), 0) + first
        if cycle:
            offsets = jnp.where(offsets < 0, offsets + cycle, offsets)
            offsets = jnp.where(offsets >= cycle, offsets - cycle, offsets)
        table = jnp.zeros((rows, cols), F32)
        for position in range(count):
            table = jnp.where(offsets == position, tap(level, member, position), table)
        return table

    def y_table(ref, level, rows, cols, first, cycle, places):
        for member in range(terms):
            high, low = halves(band(level, member, rows, cols, first, cycle, places))
            at = slice(member * rows, (member + 1) * rows)
            ref[at, 0:cols] = high
            ref[at, cols : 2 * cols] = high
            ref[at, 2 * cols : 3 * cols] = low

    def z_table(ref, level, n):
        def rows_of(i):
            start = pl.multiple_of(i * 16, 16)
            offsets = (
                lax.broadcasted_iota(jnp.int32, (16, n), 0)
                + start
                - lax.broadcasted_iota(jnp.int32, (16, n), 1)
                + radius
            )
            offsets = jnp.where(offsets < 0, offsets + n, offsets)
            offsets = jnp.where(offsets >= n, offsets - n, offsets)
            for member in range(terms):
                table = jnp.zeros((16, n), F32)
                for position in range(count):
                    table = jnp.where(offsets == position, tap(level, member, position), table)
                high, low = halves(table)
                ref[0, pl.ds(pl.multiple_of(member * n + start, 16), 16), :] = high
                ref[1, pl.ds(pl.multiple_of(member * n + start, 16), 16), :] = low

        repeat(n // 16, 1, rows_of)

    sem = [0]

    def remote(source, target, dx, dy):
        index = sem[0]
        sem[0] += 1
        return pltpu.make_async_remote_copy(
            src_ref=source, dst_ref=target, send_sem=send.at[index], recv_sem=recv.at[index],
            device_id=device(dx, dy), device_id_type=MESH,
        )

    def both(copies):
        for copy in copies:
            copy.start()
        return copies

    def arrive(copies):
        for copy in copies:
            copy.wait_recv()

    extra = radius - 8
    per = 8 // extra
    def weighted(source, i, low, high):
        total = None
        for k in range(-2, 3):
            if low <= 2 * i + k < high:
                piece = source(2 * i + k) * SPLINE[k + 2]
                total = piece if total is None else total + piece
        return total

    for copy in fetched:
        copy.wait()
    rows1, rows2 = hx + 2, ex + 3
    half2 = l2p.shape[0]
    wide1, wide2 = ry1.shape[0], ry2.shape[0]
    for i in range(rows1):
        r1[i] = dot(ry1[...], stacked2(weighted(lambda f: fine[x0 + f, 0:by], i - 1, 0, bx)))
    high, low = halves(r1[...].reshape(rows1 * wide1, bz))
    l1w[...] = (dot(high, rz1[...]) + dot(low, rz1[...])).reshape(rows1, wide1, hz)
    for i in range(rows2):
        l2y[i] = dot(ry2[...], stacked2(weighted(lambda f: l1w[f + 1], i - 1, -1, hx + 1)))
    for i in range(rows2, 2 * half2):
        l2y[i] = jnp.zeros((wide2, hz), F32)
    high, low = halves(jnp.concatenate([l2y[0:half2], l2y[half2 : 2 * half2]], axis=2).reshape(half2 * wide2, 2 * hz))
    l2p[...] = (dot(high, rz2[...]) + dot(low, rz2[...])).reshape(l2p.shape)
    pl.semaphore_wait(barrier, len(peers))
    lines = both([
        remote(l2p, seen2.at[0], 1, 0),
        remote(l2p, seen2.at[1], -1, 0),
        remote(l2p, seen2.at[2], 2, 0),
        remote(l2p, seen2.at[3], -2, 0),
    ])
    def edge_at(ref, d, i):
        return ref.at[d, i // 4, 2 * (i % 4) : 2 * (i % 4) + 2]

    first1 = (rows1 - margin - 1, 0)
    rim = []
    for d, dx in ((0, 1), (1, -1)):
        rim.append(remote(l1w.at[first1[d] : first1[d] + margin + 1, 0:hy], (low1, high1)[d], dx, 0))
        rim[-1].start()
    for i in range(margin + 1):
        for d in range(2):
            edge_at(edge, d, i)[...] = l1w[first1[d] + i, hy : hy + 2]
    rim += both([remote(edge.at[d], edge_in.at[d], dx, 0) for d, dx in ((0, 1), (1, -1))])
    g1 = bx // per
    steps = near_steps(radius)
    side = both([
        remote(fine.at[x0:x1, by - 8 : by], fine.at[x0:x1, by : by + 8], 0, 1),
        remote(fine.at[x0:x1, 0:8], fine.at[x0:x1, by + 8 : by + 16], 0, -1),
    ])
    for i in range(bx):
        g, r = i // per, extra * (i % per)
        ext[0, g, r : r + extra] = fine[x0 + i, by - radius : by - 8]
        ext[1, g, r : r + extra] = fine[x0 + i, 8:radius]

    side += both([
        remote(ext.at[0, 0:g1], got.at[0, 0:g1], 0, 1),
        remote(ext.at[1, 0:g1], got.at[1, 0:g1], 0, -1),
    ])
    def pick(first, second):
        return even * first + odd * second

    def span(start, size):
        return pl.ds(start, size)

    near = [
        both([remote(fine.at[span(pick(x1 - b, x0 + a), b - a), 0:by], fine.at[span(pick(x0 - b, x1 + a), b - a), 0:by], even - odd, 0)])
        for a, b in steps
    ]
    places2 = []
    for k in range(wy):
        at = wide2 * k
        places2 += [(at, ey * k - at), (at + ey + 2, ey * k - 3 - ey - at), (at + ey + 3, 1000)]
    y_table(ty2, 2, wide2, wy * wide2, low_y * ey + 1 + radius, wy * ey if ny <= 2 * reach + 1 else 0, places2)
    z_table(tz2, 2, ez)
    y_table(ty0, 0, by, by + 24, radius, 0, [(by, -by - 8), (by + 8, -8), (by + 16, -by - 16 - radius), (by + 16 + extra, -8 - extra), (by + 16 + 2 * extra, 1000)])
    y_table(ty1, 1, wide1, wide1 + 2 * hy, radius + 1, 0, [(hy + 1, -hy - 2), (hy + 2, 1000), (wide1, -wide1 - hy + 1), (wide1 + hy, -wide1 - 1)])
    z_table(tz0, 0, bz)
    spare = jnp.zeros((8 - 2 * extra, bz), F32)

    def unpack(rows, first):
        for n, i in enumerate(rows):
            g, r = first + n // per, extra * (n % per)
            fine[i, by + 16 : by + 16 + extra] = got[0, g, r : r + extra]
            fine[i, by + 16 + extra : by + 16 + 2 * extra] = got[1, g, r : r + extra]
            fine[i, by + 16 + 2 * extra : by + 24] = spare

    z_table(tz1, 1, hz)

    arrive(lines)
    home = radius
    pairs = cols2.shape[1]
    whole = [None] * (2 * pairs)
    for first, source in ((home, l2p), (home - ex, seen2.at[0]), (home + ex, seen2.at[1]), (home - 2 * ex, seen2.at[2]), (home + 2 * ex, seen2.at[3])):
        for r in range(rows2):
            if 0 <= first + r < rows2 + 2 * radius:
                piece = source[r % half2][:, (r // half2) * ez : (r // half2 + 1) * ez]
                whole[first + r] = piece if whole[first + r] is None else whole[first + r] + piece
    for j in range(pairs):
        top[j] = jnp.concatenate([jnp.zeros((wide2, ez), F32) if v is None else v for v in (whole[j], whole[j + pairs])], axis=1)
    if ny == 4:
        turn = 1 - 2 * lax.rem(me_y, 2)
        fan = both([remote(top, cols2.at[3], 0, 2), remote(top, cols2.at[1 - turn], 0, turn)])
    else:
        fan = both([remote(top, cols2.at[k], 0, -(low_y + k)) for k in range(wy) if low_y + k])
    cols2[-low_y] = top[...]
    def correlate_y(ref, source, table, rows, step, first=0):
        width = table.shape[0] // terms

        def one(i):
            i = i + first
            value = dot(table[...], stacked3(source[i]))
            for member in range(terms):
                ref[member, i] = value[member * width : (member + 1) * width]

        repeat(rows, step, one)

    def correlate_x(ref, source, level, rows, first, step, start=0):
        def one(i):
            i = i + start
            for member in range(terms):
                total = None
                for position in range(count):
                    piece = source[member, i + first + position] * tap(level, member, position)
                    total = piece if total is None else total + piece
                high, low = halves(total)
                at = slice(member * total.shape[1], (member + 1) * total.shape[1])
                ref[0, i, :, at] = high
                ref[1, i, :, at] = low

        repeat(rows, step, one)

    mid[:, hy:wide1] = jnp.zeros((mid.shape[0], wide1 - hy, hz), F32)
    arrive(side)
    unpack(range(x0, x1), 0)
    correlate_y(y0, fine, ty0, bx, 4, x0)
    mid[margin + 1 : margin + hx - 1, 0:wide1] = l1w[2:hx]
    arrive(rim)
    mid[0 : margin + 1, 0:hy] = low1[...]
    mid[margin + hx - 1 : margin + hx + margin, 0:hy] = high1[...]
    for i in range(margin + 1):
        for d, at in ((0, 0), (1, margin + hx - 1)):
            mid[at + i, hy : hy + 2] = edge_at(edge_in, d, i)[...]
    for i, j in ((margin - 1, 0), (margin, 1), (margin + hx - 1, hx), (margin + hx, hx + 1)):
        mid[i, 0:wide1] += l1w[j]
    left1[...] = mid[:, 1 : hy + 1, :]
    right1[:, 0:1, :] = mid[:, hy + 1 : hy + 2, :]
    right1[:, 1:hy, :] = mid[:, 0 : hy - 1, :]
    rim2 = both([
        remote(left1, mid.at[:, wide1 : wide1 + hy], 0, 1),
        remote(right1, mid.at[:, wide1 + hy : wide1 + 2 * hy], 0, -1),
    ])
    far = both([remote(fine.at[span(pick(x0, x1 - radius), radius), 0:by], fine.at[span(pick(x1, 0), radius), 0:by], odd - even, 0)])

    def correlate_z(ref, table, rows, count):
        size = count * ref.shape[2]
        high = ref[0, rows].reshape(size, ref.shape[3])
        low = ref[1, rows].reshape(size, ref.shape[3])
        return dot(high, table[0]) + dot(low, table[0]) + dot(high, table[1])

    def prolong_x(source, j, first):
        at = j - 2 * first
        if j % 2 == 0:
            c = (j // 2) - first
            return source[c - 1] * 0.125 + source[c] * 0.75 + source[c + 1] * 0.125
        c = (j - 1) // 2 - first
        return source[c] * 0.5 + source[c + 1] * 0.5

    correlate_x(s0, y0, 0, bx - 2 * radius, 0, 1, radius)
    def pack(start, size, group):
        for n in range(size):
            g, r = group + n // per, extra * (n % per)
            ext[0, g, r : r + extra] = fine[start + n, by - radius : by - 8, :]
            ext[1, g, r : r + extra] = fine[start + n, 8:radius, :]
        rows, groups = span(start, size), slice(group, group - (-size // per))
        return both([
            remote(fine.at[rows, by - 8 : by], fine.at[rows, by : by + 8], 0, 1),
            remote(fine.at[rows, 0:8], fine.at[rows, by + 8 : by + 16], 0, -1),
            remote(ext.at[0, groups], got.at[0, groups], 0, 1),
            remote(ext.at[1, groups], got.at[1, groups], 0, -1),
        ])

    parts = [(0, radius, pick(0, x1), pick(0, bx - radius))] + [
        (a, b, pick(x1 + a, x0 - b), pick(bx - radius + a, radius - b)) for a, b in steps
    ]
    groups = [g1]
    for a, b, _, _ in parts:
        groups.append(groups[-1] + -(-(b - a) // per))
    corners = []

    def relay(copies):
        part = len(corners)
        a, b, halo, _ = parts[part]
        arrive(copies)
        corners.append(pack(halo, b - a, groups[part]))

    if ny == 4:
        arrive(fan[:1])
        fan += both([remote(cols2.at[3], cols2.at[1 + turn], 0, turn)])
        arrive(fan[1:])
    else:
        arrive(fan)
    for j in range(pairs):
        value = dot(ty2[...], stacked3(jnp.concatenate([cols2[k, j] for k in range(wy)], axis=0)))
        for member in range(terms):
            y2[member, j] = value[member * wide2 : (member + 1) * wide2, 0:ez]
            y2[member, j + pairs] = value[member * wide2 : (member + 1) * wide2, ez : 2 * ez]
    correlate_x(s2, y2, 2, rows2, 0, 1)
    tx[...] = correlate_z(s2, tz2, slice(0, rows2), rows2).reshape(tx.shape)
    for j in range(hx + 2):
        ty[j] = dot(uy2[...], stacked2(prolong_x(tx, j - 1, -1)))
    high, low = halves(ty[...].reshape((hx + 2) * ty.shape[1], ez))
    lifted = dot(high, uz2[...]) + dot(low, uz2[...])

    md[...] = lifted.reshape(md.shape)
    arrive(rim2)
    correlate_y(y1, mid, ty1, hx + 2 * margin, (hx + 2 * margin) // 2)
    correlate_x(s1, y1, 1, hx + 2, 0, 1)
    relay(far)
    md[...] += correlate_z(s1, tz1, slice(0, hx + 2), hx + 2).reshape(md.shape)
    for j in range(bx):
        high, low = halves(dot(uy1[...], stacked2(prolong_x(md, j, -1))))
        my[0, j] = high
        my[1, j] = low

    stored = []

    def finish(start, size):
        rows = span(start, size)
        high = my[0, rows].reshape(size * by, hz)
        low = my[1, rows].reshape(size * by, hz)
        total = correlate_z(s0, tz0, rows, size) + dot(high, uz1[...]) + dot(low, uz1[...])
        stage[rows] = total.reshape(size, by, bz)
        stored.append(pltpu.make_async_copy(stage.at[rows], out.at[rows], store.at[len(stored)]))
        stored[-1].start()

    for copies in near:
        relay(copies)
    finish(radius, bx - 2 * radius)
    for part, (a, b, halo, target) in enumerate(parts):
        arrive(corners[part])
        unpack([halo + n for n in range(b - a)], groups[part])
        correlate_y(y0, fine, ty0, b - a, 2, halo)
        correlate_x(s0, y0, 0, b - a, 0, 1, target)
        finish(target, b - a)
    for copy in stored:
        copy.wait()
    for copy in fan + rim + side + lines + sum(near, []) + far + rim2 + sum(corners, []):
        copy.wait_send()


def near_steps(radius):
    first = min(radius, radius // 2 + radius // 2 % 2)
    return [(0, first), (first, radius)]


def hand_over(pieces, source, target, held, load, store):
    size = source.shape[0] // pieces
    reads = [pltpu.make_async_copy(source.at[i * size : (i + 1) * size], held.at[i * size : (i + 1) * size], load.at[i]) for i in range(pieces)]
    writes = [pltpu.make_async_copy(held.at[i * size : (i + 1) * size], target.at[i * size : (i + 1) * size], store.at[i]) for i in range(pieces)]
    for copy in reads:
        copy.start()
    for before, after in zip(reads, writes):
        before.wait()
        after.start()
    for copy in writes:
        copy.wait()


def cyclic_restrict(n):
    rows = np.arange(n)[:, None]
    cols = np.arange(n // 2)[None, :]
    table = np.zeros((n, n // 2), np.float32)
    for k in range(-2, 3):
        table += SPLINE[k + 2] * ((2 * cols + k) % n == rows)
    return table


def body(charges, kernel_taps):
    nx, ny = lax.axis_size("gx"), lax.axis_size("gy")
    levels, terms, count = kernel_taps.shape
    radius = count // 2
    margin = radius + 1
    bx, by, bz = charges.shape
    hx, hy, hz = bx // 2, by // 2, bz // 2
    ex, ey, ez = bx // 4, by // 4, bz // 4
    pad = 16
    wy = min(ny, 5)
    order1 = list(range(hy)) + [hy, -1] + [None] * 6
    ry1 = fixed_table(order1, list(range(by)), len(order1))
    order2 = list(range(ey)) + [ey, ey + 1, -1] + [None] * 5
    ry2 = fixed_table(order2, order1, len(order2))
    rz1, rz2 = cyclic_restrict(bz), cyclic_restrict(hz)
    wide1 = hy + 8
    wide2 = ey + 8
    uy2 = lifted_table(list(range(-1, hy + 1)), list(range(-1, ey + 2)) + [None] * (wide2 - ey - 3), wide1)
    uy1 = lifted_table(list(range(by)), list(range(-1, hy + 1)) + [None] * (wide1 - hy - 2), by)
    fixed = [twice(ry1), jnp.asarray(rz1, BF16), twice(ry2), jnp.asarray(np.kron(np.eye(2), rz2), BF16), twice(uy2),
             jnp.asarray(rz2.T, BF16), twice(uy1), jnp.asarray(rz1.T, BF16)]
    rows1, rows2 = hx + 2, ex + 3
    half2, pairs = (rows2 + 1) // 2, (rows2 + 2 * radius + 1) // 2
    extra = radius - 8
    packed = bx * extra // 8 + sum(-(-(b - a) * extra // 8) for a, b in near_steps(radius) + [(0, radius)])
    scratch = [pltpu.SMEM(kernel_taps.shape, F32)] + [pltpu.VMEM(table.shape, table.dtype) for table in fixed] + [
        pltpu.VMEM(shape, dtype)
        for shape, dtype in (
            ((bx + 2 * radius, by + 24, bz), F32),
            ((hx + 2 * margin, wide1 + 2 * hy, hz), F32),
            ((2, packed, 8, bz), F32),
            ((2, packed, 8, bz), F32),
            ((hx + 2 * margin, hy, hz), F32),
            ((hx + 2 * margin, hy, hz), F32),
            ((margin + 1, hy, hz), F32),
            ((margin + 1, hy, hz), F32),
            ((half2, wide2, 2 * ez), F32),
            ((wy, pairs, wide2, 2 * ez), F32),
            ((4, half2, wide2, 2 * ez), F32),
            ((pairs, wide2, 2 * ez), F32),
            ((terms * by, 3 * (by + 24)), BF16),
            ((terms * wide1, 3 * (wide1 + 2 * hy)), BF16),
            ((terms * wide2, 3 * wy * wide2), BF16),
            ((2, terms * bz, bz), BF16),
            ((2, terms * hz, hz), BF16),
            ((2, terms * ez, ez), BF16),
            ((terms, bx + 2 * radius, by, bz), F32),
            ((2, bx, by, terms * bz), BF16),
            ((terms, hx + 2 * margin, wide1, hz), F32),
            ((2, hx + 2, wide1, terms * hz), BF16),
            ((terms, 2 * pairs, wide2, ez), F32),
            ((2, rows2, wide2, terms * ez), BF16),
            ((rows1, wide1, bz), F32),
            ((rows1, wide1, hz), F32),
            ((2 * half2, wide2, hz), F32),
            ((rows2, wide2, ez), F32),
            ((hx + 2, wide1, ez), F32),
            ((hx + 2, wide1, hz), F32),
            ((2, bx, by, hz), BF16),
            ((2, -(-2 * (margin + 1) // 8), 8, hz), F32),
            ((2, -(-2 * (margin + 1) // 8), 8, hz), F32),
            (charges.shape, F32),
        )
    ] + [
        pltpu.SemaphoreType.DMA((48,)),
        pltpu.SemaphoreType.DMA((48,)),
        pltpu.SemaphoreType.DMA((2 + len(fixed),)),
        pltpu.SemaphoreType.DMA((8,)),
    ]
    result = pl.pallas_call(
        functools.partial(kernel, nx, ny, radius, terms),
        out_shape=jax.ShapeDtypeStruct(charges.shape, F32),
        in_specs=[pl.BlockSpec(memory_space=pltpu.HBM)] * (2 + len(fixed)),
        out_specs=pl.BlockSpec(memory_space=pltpu.HBM),
        scratch_shapes=scratch,
        compiler_params=pltpu.CompilerParams(
            collective_id=0, has_side_effects=True, vmem_limit_bytes=60 * 2**20
        ),
    )(kernel_taps, charges, *fixed)
    pieces = 8
    return pl.pallas_call(
        functools.partial(hand_over, pieces),
        out_shape=jax.ShapeDtypeStruct(charges.shape, F32),
        in_specs=[pl.BlockSpec(memory_space=pltpu.HBM)],
        out_specs=pl.BlockSpec(memory_space=pltpu.HBM),
        scratch_shapes=[
            pltpu.VMEM(charges.shape, F32),
            pltpu.SemaphoreType.DMA((pieces,)),
            pltpu.SemaphoreType.DMA((pieces,)),
        ],
        compiler_params=pltpu.CompilerParams(vmem_limit_bytes=60 * 2**20),
    )(result)


def solution(mesh):
    return jax.shard_map(
        body,
        mesh=mesh,
        in_specs=(P("gx", "gy", None), P()),
        out_specs=P("gx", "gy", None),
        check_vma=False,
    )
```

```python
import functools

import jax
import jax.numpy as jnp
import numpy as np
from jax import lax
from jax.experimental import pallas as pl
from jax.experimental.pallas import tpu as pltpu
from jax.sharding import PartitionSpec as P

SPLINE = (0.125, 0.5, 0.75, 0.5, 0.125)
F32, BF16 = jnp.float32, jnp.bfloat16
MESH = pl.DeviceIdType.MESH


def spline_at(offset):
    return SPLINE[offset + 2] if -2 <= offset <= 2 else 0.0


def fixed_table(rows, cols, width):
    table = np.zeros((width, len(cols)), np.float32)
    for a, fine in enumerate(rows):
        for b, other in enumerate(cols):
            if fine is not None and other is not None:
                table[a, b] = spline_at(other - 2 * fine)
    return table


def lifted_table(rows, cols, width):
    table = np.zeros((width, len(cols)), np.float32)
    for a, fine in enumerate(rows):
        for b, coarse in enumerate(cols):
            if coarse is not None:
                table[a, b] = spline_at(fine - 2 * coarse)
    return table


def twice(table):
    return jnp.asarray(np.concatenate([table, table], axis=1), BF16)


def halves(value):
    high = value.astype(BF16)
    return high, (value - high.astype(F32)).astype(BF16)


def dot(left, right):
    return jnp.dot(left, right, preferred_element_type=F32)


def stacked2(value):
    high, low = halves(value)
    return jnp.concatenate([high, low], axis=0)


def stacked3(value):
    high, low = halves(value)
    return jnp.concatenate([high, low, high], axis=0)


def repeat(count, step, body):
    def trip(i, carry):
        for k in range(step):
            body(i * step + k)
        return carry

    assert count % step == 0
    lax.fori_loop(0, count // step, trip, 0)


def kernel(nx, ny, radius, terms, *refs):
    given, out, held, refs = refs[:10], refs[10], refs[11:20], refs[20:]
    taps, ry1, rz1, ry2, rz2, uy2, uz2, uy1, uz1 = held
    (fine, mid, ext, got, tips, tips_in, low1, high1, l2p, cols2, seen2, top,
           ty0, ty1, ty2, tz0, tz1, tz2, y0, s0, y1, s1, y2, s2, r1, l1w, l2y, tx, ty, md, my,
     edge, edge_in, stage, part, send, recv, load, store) = refs
    bx, by, bz = given[1].shape
    x0, x1 = radius, radius + bx
    hx, hy, hz = bx // 2, by // 2, bz // 2
    ex, ey, ez = bx // 4, by // 4, bz // 4
    count = 2 * radius + 1
    margin = radius + 1
    me_x, me_y = lax.axis_index("gx"), lax.axis_index("gy")
    reach = 2
    odd = lax.rem(me_x, 2) if nx % 2 == 0 else 0
    even = 1 - odd
    wy = min(ny, 2 * reach + 1)
    low_y = -((wy - 1) // 2)

    def device(dx, dy):
        return {"gx": lax.rem(me_x + dx + nx, nx), "gy": lax.rem(me_y + dy + ny, ny)}

    peers = {}
    for dx, dy in [(-1, 0), (1, 0), (0, -1), (0, 1), (-2, 0), (2, 0)] + [
        (0, -(low_y + k)) for k in range(wy)
    ]:
        if dx % nx or dy % ny:
            peers[(dx % nx, dy % ny)] = (dx, dy)
    barrier = pltpu.get_barrier_semaphore()
    for dx, dy in peers.values():
        pl.semaphore_signal(barrier, inc=1, device_id=device(dx, dy), device_id_type=MESH)

    fetched = [
        pltpu.make_async_copy(source, target, load.at[n])
        for n, (source, target) in enumerate(zip(given, [taps, fine.at[x0:x1, 0:by]] + list(held[1:])))
    ]
    for copy in fetched:
        copy.start()

    def tap(level, member, position):
        return taps[level, member, position]

    def band(level, member, rows, cols, first, cycle, places):
        column = lax.broadcasted_iota(jnp.int32, (rows, cols), 1)
        place = column
        for start, shift in places:
            place = jnp.where(column >= start, column + shift, place)
        offsets = place - lax.broadcasted_iota(jnp.int32, (rows, cols), 0) + first
        if cycle:
            offsets = jnp.where(offsets < 0, offsets + cycle, offsets)
            offsets = jnp.where(offsets >= cycle, offsets - cycle, offsets)
        table = jnp.zeros((rows, cols), F32)
        for position in range(count):
            table = jnp.where(offsets == position, tap(level, member, position), table)
        return table

    def y_table(ref, level, rows, cols, first, cycle, places):
        for member in range(terms):
            high, low = halves(band(level, member, rows, cols, first, cycle, places))
            at = slice(member * rows, (member + 1) * rows)
            ref[at, 0:cols] = high
            ref[at, cols : 2 * cols] = high
            ref[at, 2 * cols : 3 * cols] = low

    def z_table(ref, level, n):
        def rows_of(i):
            start = pl.multiple_of(i * 16, 16)
            offsets = (
                lax.broadcasted_iota(jnp.int32, (16, n), 0)
                + start
                - lax.broadcasted_iota(jnp.int32, (16, n), 1)
                + radius
            )
            offsets = jnp.where(offsets < 0, offsets + n, offsets)
            offsets = jnp.where(offsets >= n, offsets - n, offsets)
            for member in range(terms):
                table = jnp.zeros((16, n), F32)
                for position in range(count):
                    table = jnp.where(offsets == position, tap(level, member, position), table)
                high, low = halves(table)
                ref[0, pl.ds(pl.multiple_of(member * n + start, 16), 16), :] = high
                ref[1, pl.ds(pl.multiple_of(member * n + start, 16), 16), :] = low

        repeat(n // 16, 1, rows_of)

    sem = [0]

    def remote(source, target, dx, dy):
        index = sem[0]
        sem[0] += 1
        return pltpu.make_async_remote_copy(
            src_ref=source, dst_ref=target, send_sem=send.at[index], recv_sem=recv.at[index],
            device_id=device(dx, dy), device_id_type=MESH,
        )

    def both(copies):
        for copy in copies:
            copy.start()
        return copies

    def arrive(copies):
        for copy in copies:
            copy.wait_recv()

    extra = radius - 8
    per = 8 // extra
    tip = margin - 7
    tip_per = 8 // tip
    def weighted(source, i, low, high):
        total = None
        for k in range(-2, 3):
            if low <= 2 * i + k < high:
                piece = source(2 * i + k) * SPLINE[k + 2]
                total = piece if total is None else total + piece
        return total

    for copy in fetched:
        copy.wait()
    rows1, rows2 = hx + 2, ex + 3
    half2 = l2p.shape[0]
    wide1, wide2 = ry1.shape[0], ry2.shape[0]
    for i in range(rows1):
        r1[i] = dot(ry1[...], stacked2(weighted(lambda f: fine[x0 + f, 0:by], i - 1, 0, bx)))
    high, low = halves(r1[...].reshape(rows1 * wide1, bz))
    l1w[...] = (dot(high, rz1[...]) + dot(low, rz1[...])).reshape(rows1, wide1, hz)
    for i in range(rows2):
        l2y[i] = dot(ry2[...], stacked2(weighted(lambda f: l1w[f + 1], i - 1, -1, hx + 1)))
    for i in range(rows2, 2 * half2):
        l2y[i] = jnp.zeros((wide2, hz), F32)
    high, low = halves(jnp.concatenate([l2y[0:half2], l2y[half2 : 2 * half2]], axis=2).reshape(half2 * wide2, 2 * hz))
    l2p[...] = (dot(high, rz2[...]) + dot(low, rz2[...])).reshape(l2p.shape)
    pl.semaphore_wait(barrier, len(peers))
    lines = both([
        remote(l2p, seen2.at[0], 1, 0),
        remote(l2p, seen2.at[1], -1, 0),
        remote(l2p, seen2.at[2], 2, 0),
        remote(l2p, seen2.at[3], -2, 0),
    ])
    def edge_at(ref, d, i):
        return ref.at[d, i // 4, 2 * (i % 4) : 2 * (i % 4) + 2]

    first1 = (rows1 - margin - 1, 0)
    rim = []
    for d, dx in ((0, 1), (1, -1)):
        rim.append(remote(l1w.at[first1[d] : first1[d] + margin + 1, 0:hy], (low1, high1)[d], dx, 0))
        rim[-1].start()
    for i in range(margin + 1):
        for d in range(2):
            edge_at(edge, d, i)[...] = l1w[first1[d] + i, hy : hy + 2]
    rim += both([remote(edge.at[d], edge_in.at[d], dx, 0) for d, dx in ((0, 1), (1, -1))])
    g1 = bx // per
    steps = near_steps(radius)
    side = both([
        remote(fine.at[x0:x1, by - 8 : by], fine.at[x0:x1, by : by + 8], 0, 1),
        remote(fine.at[x0:x1, 0:8], fine.at[x0:x1, by + 8 : by + 16], 0, -1),
    ])
    for i in range(bx):
        g, r = i // per, extra * (i % per)
        ext[0, g, r : r + extra] = fine[x0 + i, by - radius : by - 8]
        ext[1, g, r : r + extra] = fine[x0 + i, 8:radius]

    side += both([
        remote(ext.at[0, 0:g1], got.at[0, 0:g1], 0, 1),
        remote(ext.at[1, 0:g1], got.at[1, 0:g1], 0, -1),
    ])
    def pick(first, second):
        return even * first + odd * second

    def span(start, size):
        return pl.ds(start, size)

    near = [
        both([remote(fine.at[span(pick(x1 - b, x0 + a), b - a), 0:by], fine.at[span(pick(x0 - b, x1 + a), b - a), 0:by], even - odd, 0)])
        for a, b in steps
    ]
    places2 = []
    for k in range(wy):
        at = wide2 * k
        places2 += [(at, ey * k - at), (at + ey + 2, ey * k - 3 - ey - at), (at + ey + 3, 1000)]
    y_table(ty2, 2, wide2, wy * wide2, low_y * ey + 1 + radius, wy * ey if ny <= 2 * reach + 1 else 0, places2)
    z_table(tz2, 2, ez)
    y_table(ty0, 0, by, by + 24, radius, 0, [(by, -by - 8), (by + 8, -8), (by + 16, -by - 16 - radius), (by + 16 + extra, -8 - extra), (by + 16 + 2 * extra, 1000)])
    low, high = wide1 + 16, wide1 + 16 + tip
    y_table(ty1, 1, wide1, wide1 + 16 + 2 * tip, radius + 1, 0, [
        (hy + 1, -hy - 2), (hy + 2, 1000), (wide1, -8 - wide1), (wide1 + 8, hy - wide1 - 8), (low, -margin - low),
        (low + tip - 1, -low - tip + 1), (high, hy + 8 - high), (high + tip - 1, hy - high - tip),
    ])
    z_table(tz0, 0, bz)
    spare = jnp.zeros((8 - 2 * extra, bz), F32)

    def unpack(rows, first):
        for n, i in enumerate(rows):
            g, r = first + n // per, extra * (n % per)
            fine[i, by + 16 : by + 16 + extra] = got[0, g, r : r + extra]
            fine[i, by + 16 + extra : by + 16 + 2 * extra] = got[1, g, r : r + extra]
            fine[i, by + 16 + 2 * extra : by + 24] = spare

    z_table(tz1, 1, hz)

    arrive(lines)
    home = radius
    pairs = cols2.shape[1]
    whole = [None] * (2 * pairs)
    for first, source in ((home, l2p), (home - ex, seen2.at[0]), (home + ex, seen2.at[1]), (home - 2 * ex, seen2.at[2]), (home + 2 * ex, seen2.at[3])):
        for r in range(rows2):
            if 0 <= first + r < rows2 + 2 * radius:
                piece = source[r % half2][:, (r // half2) * ez : (r // half2 + 1) * ez]
                whole[first + r] = piece if whole[first + r] is None else whole[first + r] + piece
    for j in range(pairs):
        top[j] = jnp.concatenate([jnp.zeros((wide2, ez), F32) if v is None else v for v in (whole[j], whole[j + pairs])], axis=1)
    if ny == 4:
        turn = 1 - 2 * lax.rem(me_y, 2)
        fan = both([remote(top, cols2.at[3], 0, 2), remote(top, cols2.at[1 - turn], 0, turn)])
    else:
        fan = both([remote(top, cols2.at[k], 0, -(low_y + k)) for k in range(wy) if low_y + k])
    cols2[-low_y] = top[...]
    def correlate_y(ref, source, table, rows, step, first=0):
        width = table.shape[0] // terms

        def one(i):
            i = i + first
            value = dot(table[...], stacked3(source[i]))
            for member in range(terms):
                ref[member, i] = value[member * width : (member + 1) * width]

        repeat(rows, step, one)

    def correlate_x(ref, source, level, rows, first, step, start=0):
        def one(i):
            i = i + start
            for member in range(terms):
                total = None
                for position in range(count):
                    piece = source[member, i + first + position] * tap(level, member, position)
                    total = piece if total is None else total + piece
                high, low = halves(total)
                at = slice(member * total.shape[1], (member + 1) * total.shape[1])
                ref[0, i, :, at] = high
                ref[1, i, :, at] = low

        repeat(rows, step, one)

    mid[:, hy:wide1] = jnp.zeros((mid.shape[0], wide1 - hy, hz), F32)
    mid[margin + 1 : margin + hx - 1, 0:wide1] = l1w[2:hx]
    arrive(rim)
    mid[0 : margin + 1, 0:hy] = low1[...]
    mid[margin + hx - 1 : margin + hx + margin, 0:hy] = high1[...]
    for i in range(margin + 1):
        for d, at in ((0, 0), (1, margin + hx - 1)):
            mid[at + i, hy : hy + 2] = edge_at(edge_in, d, i)[...]
    for i, j in ((margin - 1, 0), (margin, 1), (margin + hx - 1, hx), (margin + hx, hx + 1)):
        mid[i, 0:wide1] += l1w[j]
    rim2 = both([
        remote(mid.at[:, hy - 8 : hy], mid.at[:, wide1 : wide1 + 8], 0, 1),
        remote(mid.at[:, 0:8], mid.at[:, wide1 + 8 : wide1 + 16], 0, -1),
    ])
    for i in range(mid.shape[0]):
        g, r = i // tip_per, tip * (i % tip_per)
        for d, (a, b) in enumerate(((hy - margin, hy - 8), (8, margin))):
            tips[d, g, r : r + tip - 1] = mid[i, a:b]
            tips[d, g, r + tip - 1 : r + tip] = mid[i, hy + d : hy + d + 1]
    rim2 += both([remote(tips.at[d], tips_in.at[d], 0, dy) for d, dy in ((0, 1), (1, -1))])
    far = both([remote(fine.at[span(pick(x0, x1 - radius), radius), 0:by], fine.at[span(pick(x1, 0), radius), 0:by], odd - even, 0)])

    def correlate_z(ref, table, rows, count):
        size = count * ref.shape[2]
        high = ref[0, rows].reshape(size, ref.shape[3])
        low = ref[1, rows].reshape(size, ref.shape[3])
        return dot(high, table[0]) + dot(low, table[0]) + dot(high, table[1])

    def prolong_x(source, j, first):
        at = j - 2 * first
        if j % 2 == 0:
            c = (j // 2) - first
            return source[c - 1] * 0.125 + source[c] * 0.75 + source[c + 1] * 0.125
        c = (j - 1) // 2 - first
        return source[c] * 0.5 + source[c + 1] * 0.5

    arrive(side)
    unpack(range(x0, x1), 0)
    correlate_y(y0, fine, ty0, bx, 4, x0)
    correlate_x(s0, y0, 0, bx - 2 * radius, 0, 1, radius)
    if ny == 4:
        arrive(fan[:1])
        fan = both([remote(cols2.at[3], cols2.at[1 + turn], 0, turn)]) + fan[1:] + fan[:1]
    for e in range(radius):
        for edge_of, i in ((0, e), (1, bx - 1 - e)):
            for member in range(terms):
                total = None
                for position in range(count):
                    if x0 <= i + position < x1:
                        piece = y0[member, i + position] * tap(0, member, position)
                        total = piece if total is None else total + piece
                part[edge_of, e, member] = total

    def add_halo(edge_of, a, b):
        def choose(first, last):
            return (1 - edge_of) * first + edge_of * last

        for e in range(radius - a):
            i = choose(e, bx - 1 - e)
            for member in range(terms):
                total = part[edge_of, e, member]
                for k in range(a, min(b, radius - e)):
                    weight = tap(0, member, choose(radius - 1 - k - e, radius + 1 + k + e))
                    total = total + y0[member, choose(x0 - 1 - k, x1 + k)] * weight
                if radius - e > b:
                    part[edge_of, e, member] = total
                else:
                    high, low = halves(total)
                    s0[0, i, :, member * bz : (member + 1) * bz] = high
                    s0[1, i, :, member * bz : (member + 1) * bz] = low

    def pack(start, size, group):
        for n in range(size):
            g, r = group + n // per, extra * (n % per)
            ext[0, g, r : r + extra] = fine[start + n, by - radius : by - 8, :]
            ext[1, g, r : r + extra] = fine[start + n, 8:radius, :]
        rows, groups = span(start, size), slice(group, group - (-size // per))
        return both([
            remote(fine.at[rows, by - 8 : by], fine.at[rows, by : by + 8], 0, 1),
            remote(fine.at[rows, 0:8], fine.at[rows, by + 8 : by + 16], 0, -1),
            remote(ext.at[0, groups], got.at[0, groups], 0, 1),
            remote(ext.at[1, groups], got.at[1, groups], 0, -1),
        ])

    parts = [(0, radius, pick(0, x1), pick(0, bx - radius))] + [
        (a, b, pick(x1 + a, x0 - b), pick(bx - radius + a, radius - b)) for a, b in steps
    ]
    groups = [g1]
    for a, b, _, _ in parts:
        groups.append(groups[-1] + -(-(b - a) // per))
    corners = []

    def relay(copies):
        n = len(corners)
        a, b, halo, _ = parts[n]
        arrive(copies)
        corners.append(pack(halo, b - a, groups[n]))

    arrive(fan[:2] if ny == 4 else fan)
    for j in range(pairs):
        value = dot(ty2[...], stacked3(jnp.concatenate([cols2[k, j] for k in range(wy)], axis=0)))
        for member in range(terms):
            y2[member, j] = value[member * wide2 : (member + 1) * wide2, 0:ez]
            y2[member, j + pairs] = value[member * wide2 : (member + 1) * wide2, ez : 2 * ez]
    correlate_x(s2, y2, 2, rows2, 0, 1)
    tx[...] = correlate_z(s2, tz2, slice(0, rows2), rows2).reshape(tx.shape)
    for j in range(hx + 2):
        ty[j] = dot(uy2[...], stacked2(prolong_x(tx, j - 1, -1)))
    high, low = halves(ty[...].reshape((hx + 2) * ty.shape[1], ez))
    lifted = dot(high, uz2[...]) + dot(low, uz2[...])

    md[...] = lifted.reshape(md.shape)
    arrive(rim2)
    for i in range(mid.shape[0]):
        g, r = i // tip_per, tip * (i % tip_per)
        for d in range(2):
            mid[i, wide1 + 16 + tip * d : wide1 + 16 + tip * (d + 1)] = tips_in[d, g, r : r + tip]
    correlate_y(y1, mid, ty1, hx + 2 * margin, (hx + 2 * margin) // 2)
    correlate_x(s1, y1, 1, hx + 2, 0, 1)
    relay(far)
    md[...] += correlate_z(s1, tz1, slice(0, hx + 2), hx + 2).reshape(md.shape)
    for j in range(bx):
        high, low = halves(dot(uy1[...], stacked2(prolong_x(md, j, -1))))
        my[0, j] = high
        my[1, j] = low

    stored = []

    def finish(start, size):
        rows = span(start, size)
        high = my[0, rows].reshape(size * by, hz)
        low = my[1, rows].reshape(size * by, hz)
        total = correlate_z(s0, tz0, rows, size) + dot(high, uz1[...]) + dot(low, uz1[...])
        stage[rows] = total.reshape(size, by, bz)
        stored.append(pltpu.make_async_copy(stage.at[rows], out.at[rows], store.at[len(stored)]))
        stored[-1].start()

    for copies in near:
        relay(copies)
    finish(radius, bx - 2 * radius)
    for n, (a, b, halo, target) in enumerate(parts):
        arrive(corners[n])
        unpack([halo + k for k in range(b - a)], groups[n])
        correlate_y(y0, fine, ty0, b - a, (b - a) // 2, halo)
        add_halo(even if n else odd, a, b)
        finish(target, b - a)
    for copy in stored:
        copy.wait()
    for copy in fan + rim + side + lines + sum(near, []) + far + rim2 + sum(corners, []):
        copy.wait_send()


def near_steps(radius):
    first = min(radius, radius // 2 + radius // 2 % 2)
    return [(0, first), (first, radius)]


def hand_over(pieces, source, target, held, load, store):
    size = source.shape[0] // pieces
    reads = [pltpu.make_async_copy(source.at[i * size : (i + 1) * size], held.at[i * size : (i + 1) * size], load.at[i]) for i in range(pieces)]
    writes = [pltpu.make_async_copy(held.at[i * size : (i + 1) * size], target.at[i * size : (i + 1) * size], store.at[i]) for i in range(pieces)]
    for copy in reads:
        copy.start()
    for before, after in zip(reads, writes):
        before.wait()
        after.start()
    for copy in writes:
        copy.wait()


def cyclic_restrict(n):
    rows = np.arange(n)[:, None]
    cols = np.arange(n // 2)[None, :]
    table = np.zeros((n, n // 2), np.float32)
    for k in range(-2, 3):
        table += SPLINE[k + 2] * ((2 * cols + k) % n == rows)
    return table


def body(charges, kernel_taps):
    nx, ny = lax.axis_size("gx"), lax.axis_size("gy")
    levels, terms, count = kernel_taps.shape
    radius = count // 2
    margin = radius + 1
    bx, by, bz = charges.shape
    hx, hy, hz = bx // 2, by // 2, bz // 2
    ex, ey, ez = bx // 4, by // 4, bz // 4
    pad = 16
    wy = min(ny, 5)
    order1 = list(range(hy)) + [hy, -1] + [None] * 6
    ry1 = fixed_table(order1, list(range(by)), len(order1))
    order2 = list(range(ey)) + [ey, ey + 1, -1] + [None] * 5
    ry2 = fixed_table(order2, order1, len(order2))
    rz1, rz2 = cyclic_restrict(bz), cyclic_restrict(hz)
    wide1 = hy + 8
    wide2 = ey + 8
    uy2 = lifted_table(list(range(-1, hy + 1)), list(range(-1, ey + 2)) + [None] * (wide2 - ey - 3), wide1)
    uy1 = lifted_table(list(range(by)), list(range(-1, hy + 1)) + [None] * (wide1 - hy - 2), by)
    fixed = [twice(ry1), jnp.asarray(rz1, BF16), twice(ry2), jnp.asarray(np.kron(np.eye(2), rz2), BF16), twice(uy2),
             jnp.asarray(rz2.T, BF16), twice(uy1), jnp.asarray(rz1.T, BF16)]
    rows1, rows2 = hx + 2, ex + 3
    half2, pairs = (rows2 + 1) // 2, (rows2 + 2 * radius + 1) // 2
    extra = radius - 8
    tip = margin - 7
    packed = bx * extra // 8 + sum(-(-(b - a) * extra // 8) for a, b in near_steps(radius) + [(0, radius)])
    scratch = [pltpu.SMEM(kernel_taps.shape, F32)] + [pltpu.VMEM(table.shape, table.dtype) for table in fixed] + [
        pltpu.VMEM(shape, dtype)
        for shape, dtype in (
            ((bx + 2 * radius, by + 24, bz), F32),
            ((hx + 2 * margin, wide1 + 16 + 2 * tip, hz), F32),
            ((2, packed, 8, bz), F32),
            ((2, packed, 8, bz), F32),
            ((2, -(-(hx + 2 * margin) // (8 // tip)), 8, hz), F32),
            ((2, -(-(hx + 2 * margin) // (8 // tip)), 8, hz), F32),
            ((margin + 1, hy, hz), F32),
            ((margin + 1, hy, hz), F32),
            ((half2, wide2, 2 * ez), F32),
            ((wy, pairs, wide2, 2 * ez), F32),
            ((4, half2, wide2, 2 * ez), F32),
            ((pairs, wide2, 2 * ez), F32),
            ((terms * by, 3 * (by + 24)), BF16),
            ((terms * wide1, 3 * (wide1 + 16 + 2 * tip)), BF16),
            ((terms * wide2, 3 * wy * wide2), BF16),
            ((2, terms * bz, bz), BF16),
            ((2, terms * hz, hz), BF16),
            ((2, terms * ez, ez), BF16),
            ((terms, bx + 2 * radius, by, bz), F32),
            ((2, bx, by, terms * bz), BF16),
            ((terms, hx + 2 * margin, wide1, hz), F32),
            ((2, hx + 2, wide1, terms * hz), BF16),
            ((terms, 2 * pairs, wide2, ez), F32),
            ((2, rows2, wide2, terms * ez), BF16),
            ((rows1, wide1, bz), F32),
            ((rows1, wide1, hz), F32),
            ((2 * half2, wide2, hz), F32),
            ((rows2, wide2, ez), F32),
            ((hx + 2, wide1, ez), F32),
            ((hx + 2, wide1, hz), F32),
            ((2, bx, by, hz), BF16),
            ((2, -(-2 * (margin + 1) // 8), 8, hz), F32),
            ((2, -(-2 * (margin + 1) // 8), 8, hz), F32),
            (charges.shape, F32),
            ((2, radius, terms, by, bz), F32),
        )
    ] + [
        pltpu.SemaphoreType.DMA((36,)),
        pltpu.SemaphoreType.DMA((36,)),
        pltpu.SemaphoreType.DMA((2 + len(fixed),)),
        pltpu.SemaphoreType.DMA((8,)),
    ]
    result = pl.pallas_call(
        functools.partial(kernel, nx, ny, radius, terms),
        out_shape=jax.ShapeDtypeStruct(charges.shape, F32),
        in_specs=[pl.BlockSpec(memory_space=pltpu.HBM)] * (2 + len(fixed)),
        out_specs=pl.BlockSpec(memory_space=pltpu.HBM),
        scratch_shapes=scratch,
        compiler_params=pltpu.CompilerParams(
            collective_id=0, has_side_effects=True, vmem_limit_bytes=60 * 2**20
        ),
    )(kernel_taps, charges, *fixed)
    pieces = 8
    return pl.pallas_call(
        functools.partial(hand_over, pieces),
        out_shape=jax.ShapeDtypeStruct(charges.shape, F32),
        in_specs=[pl.BlockSpec(memory_space=pltpu.HBM)],
        out_specs=pl.BlockSpec(memory_space=pltpu.HBM),
        scratch_shapes=[
            pltpu.VMEM(charges.shape, F32),
            pltpu.SemaphoreType.DMA((pieces,)),
            pltpu.SemaphoreType.DMA((pieces,)),
        ],
        compiler_params=pltpu.CompilerParams(vmem_limit_bytes=60 * 2**20),
    )(result)


def solution(mesh):
    return jax.shard_map(
        body,
        mesh=mesh,
        in_specs=(P("gx", "gy", None), P()),
        out_specs=P("gx", "gy", None),
        check_vma=False,
    )
```

```python
import functools

import jax
import jax.numpy as jnp
from jax import lax
from jax.experimental import pallas as pl
from jax.experimental.pallas import tpu as pltpu
from jax.sharding import PartitionSpec as P

SPLINE = (0.125, 0.5, 0.75, 0.5, 0.125)
F32, BF16 = jnp.float32, jnp.bfloat16
MESH = pl.DeviceIdType.MESH


def halves(value):
    high = value.astype(BF16)
    return high, (value - high.astype(F32)).astype(BF16)


def dot(left, right):
    return jnp.dot(left, right, preferred_element_type=F32)


def stacked2(value):
    high, low = halves(value)
    return jnp.concatenate([high, low], axis=0)


def stacked3(value):
    high, low = halves(value)
    return jnp.concatenate([high, low, high], axis=0)


def repeat(count, step, body):
    def trip(i, carry):
        for k in range(step):
            body(i * step + k)
        return carry

    assert count % step == 0
    lax.fori_loop(0, count // step, trip, 0)


def kernel(nx, ny, radius, terms, *refs):
    given, out, held, refs = refs[:2], refs[2], refs[3:12], refs[12:]
    taps, ry1, rz1, ry2, rz2, uy2, uz2, uy1, uz1 = held
    (fine, mid, ext, got, tips, tips_in, low1, high1, l2p, cols2, seen2, top,
           ty0, ty1, ty2, tz0, tz1, tz2, y0, s0, y1, s1, y2, s2, r1, l1w, l2y, tx, ty, md, my,
     edge, edge_in, part, send, recv, load) = refs
    bx, by, bz = given[1].shape
    x0, x1 = radius, radius + bx
    hx, hy, hz = bx // 2, by // 2, bz // 2
    ex, ey, ez = bx // 4, by // 4, bz // 4
    count = 2 * radius + 1
    margin = radius + 1
    me_x, me_y = lax.axis_index("gx"), lax.axis_index("gy")
    reach = 2
    odd = lax.rem(me_x, 2) if nx % 2 == 0 else 0
    even = 1 - odd
    wy = min(ny, 2 * reach + 1)
    low_y = -((wy - 1) // 2)

    def device(dx, dy):
        return {"gx": lax.rem(me_x + dx + nx, nx), "gy": lax.rem(me_y + dy + ny, ny)}

    peers = {}
    for dx, dy in [(-1, 0), (1, 0), (0, -1), (0, 1), (-2, 0), (2, 0)] + [
        (0, -(low_y + k)) for k in range(wy)
    ]:
        if dx % nx or dy % ny:
            peers[(dx % nx, dy % ny)] = (dx, dy)
    barrier = pltpu.get_barrier_semaphore()
    for dx, dy in peers.values():
        pl.semaphore_signal(barrier, inc=1, device_id=device(dx, dy), device_id_type=MESH)

    fetched = [
        pltpu.make_async_copy(source, target, load.at[n])
        for n, (source, target) in enumerate(zip(given, [taps, fine.at[x0:x1, 0:by]]))
    ]
    for copy in fetched:
        copy.start()

    def tap(level, member, position):
        return taps[level, member, position]

    def band(level, member, rows, cols, first, cycle, places):
        column = lax.broadcasted_iota(jnp.int32, (rows, cols), 1)
        place = column
        for start, shift in places:
            place = jnp.where(column >= start, column + shift, place)
        offsets = place - lax.broadcasted_iota(jnp.int32, (rows, cols), 0) + first
        if cycle:
            offsets = jnp.where(offsets < 0, offsets + cycle, offsets)
            offsets = jnp.where(offsets >= cycle, offsets - cycle, offsets)
        table = jnp.zeros((rows, cols), F32)
        for position in range(count):
            table = jnp.where(offsets == position, tap(level, member, position), table)
        return table

    def y_table(ref, level, rows, cols, first, cycle, places):
        for member in range(terms):
            high, low = halves(band(level, member, rows, cols, first, cycle, places))
            at = slice(member * rows, (member + 1) * rows)
            ref[at, 0:cols] = high
            ref[at, cols : 2 * cols] = high
            ref[at, 2 * cols : 3 * cols] = low

    def z_table(ref, level, n):
        def rows_of(i):
            start = pl.multiple_of(i * 16, 16)
            offsets = (
                lax.broadcasted_iota(jnp.int32, (16, n), 0)
                + start
                - lax.broadcasted_iota(jnp.int32, (16, n), 1)
                + radius
            )
            offsets = jnp.where(offsets < 0, offsets + n, offsets)
            offsets = jnp.where(offsets >= n, offsets - n, offsets)
            for member in range(terms):
                table = jnp.zeros((16, n), F32)
                for position in range(count):
                    table = jnp.where(offsets == position, tap(level, member, position), table)
                high, low = halves(table)
                ref[0, pl.ds(pl.multiple_of(member * n + start, 16), 16), :] = high
                ref[1, pl.ds(pl.multiple_of(member * n + start, 16), 16), :] = low

        repeat(n // 16, 1, rows_of)

    sem = [0]

    def remote(source, target, dx, dy):
        index = sem[0]
        sem[0] += 1
        return pltpu.make_async_remote_copy(
            src_ref=source, dst_ref=target, send_sem=send.at[index], recv_sem=recv.at[index],
            device_id=device(dx, dy), device_id_type=MESH,
        )

    def both(copies):
        for copy in copies:
            copy.start()
        return copies

    def arrive(copies):
        for copy in copies:
            copy.wait_recv()

    extra = radius - 8
    per = 8 // extra
    tip = margin - 7
    tip_per = 8 // tip
    def weighted(source, i, low, high):
        total = None
        for k in range(-2, 3):
            if low <= 2 * i + k < high:
                piece = source(2 * i + k) * SPLINE[k + 2]
                total = piece if total is None else total + piece
        return total

    def places(shape, axis):
        return lax.broadcasted_iota(jnp.int32, shape, axis)

    def spline_table(ref, offset, valid):
        distance = jnp.abs(offset)
        value = jnp.where(distance == 0, SPLINE[2], jnp.where(distance == 1, SPLINE[1], jnp.where(distance == 2, SPLINE[0], 0.0)))
        ref[...] = jnp.where(valid, value, 0.0).astype(BF16)

    def folded(index, width):
        return jnp.where(index >= width, index - width, index)

    def along_z(ref, fine_axis, n, blocks):
        rows, cols = places(ref.shape, fine_axis), places(ref.shape, 1 - fine_axis)
        same = (rows >= n) == (cols >= n // 2) if blocks == 2 else rows >= 0
        offset = folded(rows, n) - 2 * folded(cols, n // 2) if blocks == 2 else rows - 2 * cols
        offset = jnp.where(offset > n // 2, offset - n, jnp.where(offset < -(n // 2), offset + n, offset))
        spline_table(ref, offset, same)

    a, b = places(ry1.shape, 0), folded(places(ry1.shape, 1), by)
    spline_table(ry1, b - 2 * jnp.where(a == hy + 1, -1, a), a <= hy + 1)
    a, b = places(ry2.shape, 0), folded(places(ry2.shape, 1), ry1.shape[0])
    spline_table(ry2, jnp.where(b == hy + 1, -1, b) - 2 * jnp.where(a == ey + 2, -1, a), (a <= ey + 2) & (b <= hy + 1))
    a, b = places(uy2.shape, 0), folded(places(uy2.shape, 1), ry2.shape[0])
    spline_table(uy2, a + 1 - 2 * b, (a < hy + 2) & (b < ey + 3))
    a, b = places(uy1.shape, 0), folded(places(uy1.shape, 1), ry1.shape[0])
    spline_table(uy1, a + 2 - 2 * b, b < hy + 2)
    along_z(rz1, 0, bz, 1)
    along_z(uz1, 1, bz, 1)
    along_z(rz2, 0, hz, 2)
    along_z(uz2, 1, hz, 1)
    for copy in fetched:
        copy.wait()
    rows1, rows2 = hx + 2, ex + 3
    half2 = l2p.shape[0]
    wide1, wide2 = ry1.shape[0], ry2.shape[0]
    for i in range(rows1):
        r1[i] = dot(ry1[...], stacked2(weighted(lambda f: fine[x0 + f, 0:by], i - 1, 0, bx)))
    high, low = halves(r1[...].reshape(rows1 * wide1, bz))
    l1w[...] = (dot(high, rz1[...]) + dot(low, rz1[...])).reshape(rows1, wide1, hz)
    for i in range(rows2):
        l2y[i] = dot(ry2[...], stacked2(weighted(lambda f: l1w[f + 1], i - 1, -1, hx + 1)))
    for i in range(rows2, 2 * half2):
        l2y[i] = jnp.zeros((wide2, hz), F32)
    high, low = halves(jnp.concatenate([l2y[0:half2], l2y[half2 : 2 * half2]], axis=2).reshape(half2 * wide2, 2 * hz))
    l2p[...] = (dot(high, rz2[...]) + dot(low, rz2[...])).reshape(l2p.shape)
    pl.semaphore_wait(barrier, len(peers))
    lines = both([
        remote(l2p, seen2.at[0], 1, 0),
        remote(l2p, seen2.at[1], -1, 0),
        remote(l2p, seen2.at[2], 2, 0),
        remote(l2p, seen2.at[3], -2, 0),
    ])
    def edge_at(ref, d, i):
        return ref.at[d, i // 4, 2 * (i % 4) : 2 * (i % 4) + 2]

    first1 = (rows1 - margin - 1, 0)
    rim = []
    for d, dx in ((0, 1), (1, -1)):
        rim.append(remote(l1w.at[first1[d] : first1[d] + margin + 1, 0:hy], (low1, high1)[d], dx, 0))
        rim[-1].start()
    for i in range(margin + 1):
        for d in range(2):
            edge_at(edge, d, i)[...] = l1w[first1[d] + i, hy : hy + 2]
    rim += both([remote(edge.at[d], edge_in.at[d], dx, 0) for d, dx in ((0, 1), (1, -1))])
    g1 = bx // per
    steps = near_steps(radius)
    side = both([
        remote(fine.at[x0:x1, by - 8 : by], fine.at[x0:x1, by : by + 8], 0, 1),
        remote(fine.at[x0:x1, 0:8], fine.at[x0:x1, by + 8 : by + 16], 0, -1),
    ])
    for i in range(bx):
        g, r = i // per, extra * (i % per)
        ext[0, g, r : r + extra] = fine[x0 + i, by - radius : by - 8]
        ext[1, g, r : r + extra] = fine[x0 + i, 8:radius]

    side += both([
        remote(ext.at[0, 0:g1], got.at[0, 0:g1], 0, 1),
        remote(ext.at[1, 0:g1], got.at[1, 0:g1], 0, -1),
    ])
    def pick(first, second):
        return even * first + odd * second

    def span(start, size):
        return pl.ds(start, size)

    near = [
        both([remote(fine.at[span(pick(x1 - b, x0 + a), b - a), 0:by], fine.at[span(pick(x0 - b, x1 + a), b - a), 0:by], even - odd, 0)])
        for a, b in steps
    ]
    places2 = []
    for k in range(wy):
        at = wide2 * k
        places2 += [(at, ey * k - at), (at + ey + 2, ey * k - 3 - ey - at), (at + ey + 3, 1000)]
    y_table(ty2, 2, wide2, wy * wide2, low_y * ey + 1 + radius, wy * ey if ny <= 2 * reach + 1 else 0, places2)
    z_table(tz2, 2, ez)
    y_table(ty0, 0, by, by + 24, radius, 0, [(by, -by - 8), (by + 8, -8), (by + 16, -by - 16 - radius), (by + 16 + extra, -8 - extra), (by + 16 + 2 * extra, 1000)])
    low, high = wide1 + 16, wide1 + 16 + tip
    y_table(ty1, 1, wide1, wide1 + 16 + 2 * tip, radius + 1, 0, [
        (hy + 1, -hy - 2), (hy + 2, 1000), (wide1, -8 - wide1), (wide1 + 8, hy - wide1 - 8), (low, -margin - low),
        (low + tip - 1, -low - tip + 1), (high, hy + 8 - high), (high + tip - 1, hy - high - tip),
    ])
    z_table(tz0, 0, bz)
    spare = jnp.zeros((8 - 2 * extra, bz), F32)

    def unpack(rows, first):
        for n, i in enumerate(rows):
            g, r = first + n // per, extra * (n % per)
            fine[i, by + 16 : by + 16 + extra] = got[0, g, r : r + extra]
            fine[i, by + 16 + extra : by + 16 + 2 * extra] = got[1, g, r : r + extra]
            fine[i, by + 16 + 2 * extra : by + 24] = spare

    z_table(tz1, 1, hz)

    arrive(lines)
    home = radius
    pairs = cols2.shape[1]
    whole = [None] * (2 * pairs)
    for first, source in ((home, l2p), (home - ex, seen2.at[0]), (home + ex, seen2.at[1]), (home - 2 * ex, seen2.at[2]), (home + 2 * ex, seen2.at[3])):
        for r in range(rows2):
            if 0 <= first + r < rows2 + 2 * radius:
                piece = source[r % half2][:, (r // half2) * ez : (r // half2 + 1) * ez]
                whole[first + r] = piece if whole[first + r] is None else whole[first + r] + piece
    for j in range(pairs):
        top[j] = jnp.concatenate([jnp.zeros((wide2, ez), F32) if v is None else v for v in (whole[j], whole[j + pairs])], axis=1)
    if ny == 4:
        turn = 1 - 2 * lax.rem(me_y, 2)
        fan = both([remote(top, cols2.at[3], 0, 2), remote(top, cols2.at[1 - turn], 0, turn)])
    else:
        fan = both([remote(top, cols2.at[k], 0, -(low_y + k)) for k in range(wy) if low_y + k])
    cols2[-low_y] = top[...]
    def correlate_y(ref, source, table, rows, step, first=0):
        width = table.shape[0] // terms

        def one(i):
            i = i + first
            value = dot(table[...], stacked3(source[i]))
            for member in range(terms):
                ref[member, i] = value[member * width : (member + 1) * width]

        repeat(rows, step, one)

    def correlate_x(ref, source, level, rows, first, step, start=0):
        def one(i):
            i = i + start
            for member in range(terms):
                total = None
                for position in range(count):
                    piece = source[member, i + first + position] * tap(level, member, position)
                    total = piece if total is None else total + piece
                high, low = halves(total)
                at = slice(member * total.shape[1], (member + 1) * total.shape[1])
                ref[0, i, :, at] = high
                ref[1, i, :, at] = low

        repeat(rows, step, one)

    mid[:, hy:wide1] = jnp.zeros((mid.shape[0], wide1 - hy, hz), F32)
    mid[margin + 1 : margin + hx - 1, 0:wide1] = l1w[2:hx]
    arrive(rim)
    mid[0 : margin + 1, 0:hy] = low1[...]
    mid[margin + hx - 1 : margin + hx + margin, 0:hy] = high1[...]
    for i in range(margin + 1):
        for d, at in ((0, 0), (1, margin + hx - 1)):
            mid[at + i, hy : hy + 2] = edge_at(edge_in, d, i)[...]
    for i, j in ((margin - 1, 0), (margin, 1), (margin + hx - 1, hx), (margin + hx, hx + 1)):
        mid[i, 0:wide1] += l1w[j]
    rim2 = both([
        remote(mid.at[:, hy - 8 : hy], mid.at[:, wide1 : wide1 + 8], 0, 1),
        remote(mid.at[:, 0:8], mid.at[:, wide1 + 8 : wide1 + 16], 0, -1),
    ])
    for i in range(mid.shape[0]):
        g, r = i // tip_per, tip * (i % tip_per)
        for d, (a, b) in enumerate(((hy - margin, hy - 8), (8, margin))):
            tips[d, g, r : r + tip - 1] = mid[i, a:b]
            tips[d, g, r + tip - 1 : r + tip] = mid[i, hy + d : hy + d + 1]
    rim2 += both([remote(tips.at[d], tips_in.at[d], 0, dy) for d, dy in ((0, 1), (1, -1))])
    far = both([remote(fine.at[span(pick(x0, x1 - radius), radius), 0:by], fine.at[span(pick(x1, 0), radius), 0:by], odd - even, 0)])

    def correlate_z(ref, table, rows, count):
        size = count * ref.shape[2]
        high = ref[0, rows].reshape(size, ref.shape[3])
        low = ref[1, rows].reshape(size, ref.shape[3])
        return dot(high, table[0]) + dot(low, table[0]) + dot(high, table[1])

    def prolong_x(source, j, first):
        at = j - 2 * first
        if j % 2 == 0:
            c = (j // 2) - first
            return source[c - 1] * 0.125 + source[c] * 0.75 + source[c + 1] * 0.125
        c = (j - 1) // 2 - first
        return source[c] * 0.5 + source[c + 1] * 0.5

    arrive(side)
    unpack(range(x0, x1), 0)
    correlate_y(y0, fine, ty0, bx, 4, x0)
    correlate_x(s0, y0, 0, bx - 2 * radius, 0, 1, radius)
    if ny == 4:
        arrive(fan[:1])
        fan = both([remote(cols2.at[3], cols2.at[1 + turn], 0, turn)]) + fan[1:] + fan[:1]
    for e in range(radius):
        for edge_of, i in ((0, e), (1, bx - 1 - e)):
            for member in range(terms):
                total = None
                for position in range(count):
                    if x0 <= i + position < x1:
                        piece = y0[member, i + position] * tap(0, member, position)
                        total = piece if total is None else total + piece
                part[edge_of, e, member] = total

    def add_halo(edge_of, a, b):
        def choose(first, last):
            return (1 - edge_of) * first + edge_of * last

        for e in range(radius - a):
            i = choose(e, bx - 1 - e)
            for member in range(terms):
                total = part[edge_of, e, member]
                for k in range(a, min(b, radius - e)):
                    weight = tap(0, member, choose(radius - 1 - k - e, radius + 1 + k + e))
                    total = total + y0[member, choose(x0 - 1 - k, x1 + k)] * weight
                if radius - e > b:
                    part[edge_of, e, member] = total
                else:
                    high, low = halves(total)
                    s0[0, i, :, member * bz : (member + 1) * bz] = high
                    s0[1, i, :, member * bz : (member + 1) * bz] = low

    def pack(start, size, group):
        for n in range(size):
            g, r = group + n // per, extra * (n % per)
            ext[0, g, r : r + extra] = fine[start + n, by - radius : by - 8, :]
            ext[1, g, r : r + extra] = fine[start + n, 8:radius, :]
        rows, groups = span(start, size), slice(group, group - (-size // per))
        return both([
            remote(fine.at[rows, by - 8 : by], fine.at[rows, by : by + 8], 0, 1),
            remote(fine.at[rows, 0:8], fine.at[rows, by + 8 : by + 16], 0, -1),
            remote(ext.at[0, groups], got.at[0, groups], 0, 1),
            remote(ext.at[1, groups], got.at[1, groups], 0, -1),
        ])

    parts = [(0, radius, pick(0, x1), pick(0, bx - radius))] + [
        (a, b, pick(x1 + a, x0 - b), pick(bx - radius + a, radius - b)) for a, b in steps
    ]
    groups = [g1]
    for a, b, _, _ in parts:
        groups.append(groups[-1] + -(-(b - a) // per))
    corners = []

    def relay(copies):
        n = len(corners)
        a, b, halo, _ = parts[n]
        arrive(copies)
        corners.append(pack(halo, b - a, groups[n]))

    arrive(fan[:2] if ny == 4 else fan)
    for j in range(pairs):
        value = dot(ty2[...], stacked3(jnp.concatenate([cols2[k, j] for k in range(wy)], axis=0)))
        for member in range(terms):
            y2[member, j] = value[member * wide2 : (member + 1) * wide2, 0:ez]
            y2[member, j + pairs] = value[member * wide2 : (member + 1) * wide2, ez : 2 * ez]
    correlate_x(s2, y2, 2, rows2, 0, 1)
    tx[...] = correlate_z(s2, tz2, slice(0, rows2), rows2).reshape(tx.shape)
    for j in range(hx + 2):
        ty[j] = dot(uy2[...], stacked2(prolong_x(tx, j - 1, -1)))
    high, low = halves(ty[...].reshape((hx + 2) * ty.shape[1], ez))
    lifted = dot(high, uz2[...]) + dot(low, uz2[...])

    md[...] = lifted.reshape(md.shape)
    arrive(rim2)
    for i in range(mid.shape[0]):
        g, r = i // tip_per, tip * (i % tip_per)
        for d in range(2):
            mid[i, wide1 + 16 + tip * d : wide1 + 16 + tip * (d + 1)] = tips_in[d, g, r : r + tip]
    correlate_y(y1, mid, ty1, hx + 2 * margin, (hx + 2 * margin) // 2)
    correlate_x(s1, y1, 1, hx + 2, 0, 1)
    relay(far)
    md[...] += correlate_z(s1, tz1, slice(0, hx + 2), hx + 2).reshape(md.shape)
    for j in range(bx):
        high, low = halves(dot(uy1[...], stacked2(prolong_x(md, j, -1))))
        my[0, j] = high
        my[1, j] = low

    def finish(start, size):
        rows = span(start, size)
        high = my[0, rows].reshape(size * by, hz)
        low = my[1, rows].reshape(size * by, hz)
        total = correlate_z(s0, tz0, rows, size) + dot(high, uz1[...]) + dot(low, uz1[...])
        out[rows] = total.reshape(size, by, bz)

    for copies in near:
        relay(copies)
    finish(radius, bx - 2 * radius)
    for n, (a, b, halo, target) in enumerate(parts):
        arrive(corners[n])
        unpack([halo + k for k in range(b - a)], groups[n])
        correlate_y(y0, fine, ty0, b - a, (b - a) // 2, halo)
        add_halo(even if n else odd, a, b)
        finish(target, b - a)
    for copy in fan + rim + side + lines + sum(near, []) + far + rim2 + sum(corners, []):
        copy.wait_send()


def near_steps(radius):
    first = min(radius, radius // 2 + radius // 2 % 2)
    return [(0, first), (first, radius)]


def body(charges, kernel_taps):
    nx, ny = lax.axis_size("gx"), lax.axis_size("gy")
    levels, terms, count = kernel_taps.shape
    radius = count // 2
    margin = radius + 1
    bx, by, bz = charges.shape
    hx, hy, hz = bx // 2, by // 2, bz // 2
    ex, ey, ez = bx // 4, by // 4, bz // 4
    wy = min(ny, 5)
    wide1 = hy + 8
    wide2 = ey + 8
    tables = [(wide1, 2 * by), (bz, hz), (wide2, 2 * wide1), (2 * hz, 2 * ez), (wide1, 2 * wide2), (ez, hz), (by, 2 * wide1), (hz, bz)]
    rows1, rows2 = hx + 2, ex + 3
    half2, pairs = (rows2 + 1) // 2, (rows2 + 2 * radius + 1) // 2
    extra = radius - 8
    tip = margin - 7
    packed = bx * extra // 8 + sum(-(-(b - a) * extra // 8) for a, b in near_steps(radius) + [(0, radius)])
    scratch = [pltpu.SMEM(kernel_taps.shape, F32)] + [pltpu.VMEM(shape, BF16) for shape in tables] + [
        pltpu.VMEM(shape, dtype)
        for shape, dtype in (
            ((bx + 2 * radius, by + 24, bz), F32),
            ((hx + 2 * margin, wide1 + 16 + 2 * tip, hz), F32),
            ((2, packed, 8, bz), F32),
            ((2, packed, 8, bz), F32),
            ((2, -(-(hx + 2 * margin) // (8 // tip)), 8, hz), F32),
            ((2, -(-(hx + 2 * margin) // (8 // tip)), 8, hz), F32),
            ((margin + 1, hy, hz), F32),
            ((margin + 1, hy, hz), F32),
            ((half2, wide2, 2 * ez), F32),
            ((wy, pairs, wide2, 2 * ez), F32),
            ((4, half2, wide2, 2 * ez), F32),
            ((pairs, wide2, 2 * ez), F32),
            ((terms * by, 3 * (by + 24)), BF16),
            ((terms * wide1, 3 * (wide1 + 16 + 2 * tip)), BF16),
            ((terms * wide2, 3 * wy * wide2), BF16),
            ((2, terms * bz, bz), BF16),
            ((2, terms * hz, hz), BF16),
            ((2, terms * ez, ez), BF16),
            ((terms, bx + 2 * radius, by, bz), F32),
            ((2, bx, by, terms * bz), BF16),
            ((terms, hx + 2 * margin, wide1, hz), F32),
            ((2, hx + 2, wide1, terms * hz), BF16),
            ((terms, 2 * pairs, wide2, ez), F32),
            ((2, rows2, wide2, terms * ez), BF16),
            ((rows1, wide1, bz), F32),
            ((rows1, wide1, hz), F32),
            ((2 * half2, wide2, hz), F32),
            ((rows2, wide2, ez), F32),
            ((hx + 2, wide1, ez), F32),
            ((hx + 2, wide1, hz), F32),
            ((2, bx, by, hz), BF16),
            ((2, -(-2 * (margin + 1) // 8), 8, hz), F32),
            ((2, -(-2 * (margin + 1) // 8), 8, hz), F32),
            ((2, radius, terms, by, bz), F32),
        )
    ] + [
        pltpu.SemaphoreType.DMA((36,)),
        pltpu.SemaphoreType.DMA((36,)),
        pltpu.SemaphoreType.DMA((2,)),
    ]
    result = pl.pallas_call(
        functools.partial(kernel, nx, ny, radius, terms),
        out_shape=jax.ShapeDtypeStruct(charges.shape, F32),
        in_specs=[pl.BlockSpec(memory_space=pltpu.HBM)] * 2,
        out_specs=pl.BlockSpec(memory_space=pltpu.VMEM),
        scratch_shapes=scratch,
        compiler_params=pltpu.CompilerParams(
            collective_id=0, has_side_effects=True, vmem_limit_bytes=211 * 2**18
        ),
    )(kernel_taps, charges)
    return result


def solution(mesh):
    return jax.shard_map(
        body,
        mesh=mesh,
        in_specs=(P("gx", "gy", None), P()),
        out_specs=P("gx", "gy", None),
        check_vma=False,
    )
```

```python
import functools

import jax
import jax.numpy as jnp
from jax import lax
from jax.experimental import pallas as pl
from jax.experimental.pallas import tpu as pltpu
from jax.sharding import PartitionSpec as P

SPLINE = (0.125, 0.5, 0.75, 0.5, 0.125)
F32, BF16 = jnp.float32, jnp.bfloat16
MESH = pl.DeviceIdType.MESH


def halves(value):
    high = value.astype(BF16)
    return high, (value - high.astype(F32)).astype(BF16)


def dot(left, right):
    return jnp.dot(left, right, preferred_element_type=F32)


def stacked2(value):
    high, low = halves(value)
    return jnp.concatenate([high, low], axis=0)


def stacked3(value):
    high, low = halves(value)
    return jnp.concatenate([high, low, high], axis=0)


def repeat(count, step, body):
    def trip(i, carry):
        for k in range(step):
            body(i * step + k)
        return carry

    assert count % step == 0
    lax.fori_loop(0, count // step, trip, 0)


def kernel(nx, ny, radius, terms, *refs):
    given, out, held, refs = refs[:2], refs[2], refs[3:12], refs[12:]
    taps, ry1, rz1, ry2, rz2, uy2, uz2, uy1, uz1 = held
    (fine, mid, ext, got, tips, tips_in, low1, high1, l2p, cols2, seen2, top,
           ty0, ty1, ty2, tz0, tz1, tz2, y0, s0, y1, s1, y2, s2, r1, l1w, l2y, tx, ty, md, my,
     edge, edge_in, part, send, recv, load) = refs
    bx, by, bz = given[1].shape
    x0, x1 = radius, radius + bx
    hx, hy, hz = bx // 2, by // 2, bz // 2
    ex, ey, ez = bx // 4, by // 4, bz // 4
    count = 2 * radius + 1
    margin = radius + 1
    me_x, me_y = lax.axis_index("gx"), lax.axis_index("gy")
    reach = 2
    odd = lax.rem(me_x, 2) if nx % 2 == 0 else 0
    even = 1 - odd
    wy = min(ny, 2 * reach + 1)
    low_y = -((wy - 1) // 2)

    def device(dx, dy):
        return {"gx": lax.rem(me_x + dx + nx, nx), "gy": lax.rem(me_y + dy + ny, ny)}

    peers = {}
    for dx, dy in [(-1, 0), (1, 0), (0, -1), (0, 1), (-2, 0), (2, 0)] + [
        (0, -(low_y + k)) for k in range(wy)
    ]:
        if dx % nx or dy % ny:
            peers[(dx % nx, dy % ny)] = (dx, dy)
    barrier = pltpu.get_barrier_semaphore()
    for dx, dy in peers.values():
        pl.semaphore_signal(barrier, inc=1, device_id=device(dx, dy), device_id_type=MESH)

    fetched = [
        pltpu.make_async_copy(source, target, load.at[n])
        for n, (source, target) in enumerate(zip(given, [taps, fine.at[x0:x1, 0:by]]))
    ]
    for copy in fetched:
        copy.start()

    def tap(level, member, position):
        return taps[level, member, position]

    def band(level, member, rows, cols, first, cycle, places):
        column = lax.broadcasted_iota(jnp.int32, (rows, cols), 1)
        place = column
        for start, shift in places:
            place = jnp.where(column >= start, column + shift, place)
        offsets = place - lax.broadcasted_iota(jnp.int32, (rows, cols), 0) + first
        if cycle:
            offsets = jnp.where(offsets < 0, offsets + cycle, offsets)
            offsets = jnp.where(offsets >= cycle, offsets - cycle, offsets)
        table = jnp.zeros((rows, cols), F32)
        for position in range(count):
            table = jnp.where(offsets == position, tap(level, member, position), table)
        return table

    def y_table(ref, level, rows, cols, first, cycle, places):
        for member in range(terms):
            high, low = halves(band(level, member, rows, cols, first, cycle, places))
            at = slice(member * rows, (member + 1) * rows)
            ref[at, 0:cols] = high
            ref[at, cols : 2 * cols] = high
            ref[at, 2 * cols : 3 * cols] = low

    def z_table(ref, level, n):
        def rows_of(i):
            start = pl.multiple_of(i * 16, 16)
            offsets = (
                lax.broadcasted_iota(jnp.int32, (16, n), 0)
                + start
                - lax.broadcasted_iota(jnp.int32, (16, n), 1)
                + radius
            )
            offsets = jnp.where(offsets < 0, offsets + n, offsets)
            offsets = jnp.where(offsets >= n, offsets - n, offsets)
            for member in range(terms):
                table = jnp.zeros((16, n), F32)
                for position in range(count):
                    table = jnp.where(offsets == position, tap(level, member, position), table)
                high, low = halves(table)
                ref[0, pl.ds(pl.multiple_of(member * n + start, 16), 16), :] = high
                ref[1, pl.ds(pl.multiple_of(member * n + start, 16), 16), :] = low

        repeat(n // 16, 1, rows_of)

    sem = [0]

    def remote(source, target, dx, dy):
        index = sem[0]
        sem[0] += 1
        return pltpu.make_async_remote_copy(
            src_ref=source, dst_ref=target, send_sem=send.at[index], recv_sem=recv.at[index],
            device_id=device(dx, dy), device_id_type=MESH,
        )

    def both(copies):
        for copy in copies:
            copy.start()
        return copies

    def arrive(copies):
        for copy in copies:
            copy.wait_recv()

    extra = radius - 8
    per = 8 // extra
    tip = margin - 7
    tip_per = 8 // tip
    def weighted(source, i, low, high):
        total = None
        for k in range(-2, 3):
            if low <= 2 * i + k < high:
                piece = source(2 * i + k) * SPLINE[k + 2]
                total = piece if total is None else total + piece
        return total

    def places(shape, axis):
        return lax.broadcasted_iota(jnp.int32, shape, axis)

    def spline_table(ref, offset, valid):
        distance = jnp.abs(offset)
        value = jnp.where(distance == 0, SPLINE[2], jnp.where(distance == 1, SPLINE[1], jnp.where(distance == 2, SPLINE[0], 0.0)))
        ref[...] = jnp.where(valid, value, 0.0).astype(BF16)

    def folded(index, width):
        return jnp.where(index >= width, index - width, index)

    def along_z(ref, fine_axis, n, blocks):
        rows, cols = places(ref.shape, fine_axis), places(ref.shape, 1 - fine_axis)
        same = (rows >= n) == (cols >= n // 2) if blocks == 2 else rows >= 0
        offset = folded(rows, n) - 2 * folded(cols, n // 2) if blocks == 2 else rows - 2 * cols
        offset = jnp.where(offset > n // 2, offset - n, jnp.where(offset < -(n // 2), offset + n, offset))
        spline_table(ref, offset, same)

    a, b = places(ry1.shape, 0), folded(places(ry1.shape, 1), by)
    spline_table(ry1, b - 2 * jnp.where(a == hy + 1, -1, a), a <= hy + 1)
    a, b = places(ry2.shape, 0), folded(places(ry2.shape, 1), ry1.shape[0])
    spline_table(ry2, jnp.where(b == hy + 1, -1, b) - 2 * jnp.where(a == ey + 2, -1, a), (a <= ey + 2) & (b <= hy + 1))
    a, b = places(uy2.shape, 0), folded(places(uy2.shape, 1), ry2.shape[0])
    spline_table(uy2, a + 1 - 2 * b, (a < hy + 2) & (b < ey + 3))
    a, b = places(uy1.shape, 0), folded(places(uy1.shape, 1), ry1.shape[0])
    spline_table(uy1, a + 2 - 2 * b, b < hy + 2)
    along_z(rz1, 0, bz, 1)
    along_z(uz1, 1, bz, 1)
    along_z(rz2, 0, hz, 2)
    along_z(uz2, 1, hz, 1)
    for copy in fetched:
        copy.wait()
    rows1, rows2 = hx + 2, ex + 3
    half2 = l2p.shape[0]
    wide1, wide2 = ry1.shape[0], ry2.shape[0]
    for i in range(rows1):
        r1[i] = dot(ry1[...], stacked2(weighted(lambda f: fine[x0 + f, 0:by], i - 1, 0, bx)))
    high, low = halves(r1[...].reshape(rows1 * wide1, bz))
    l1w[...] = (dot(high, rz1[...]) + dot(low, rz1[...])).reshape(rows1, wide1, hz)
    for i in range(rows2):
        l2y[i] = dot(ry2[...], stacked2(weighted(lambda f: l1w[f + 1], i - 1, -1, hx + 1)))
    for i in range(rows2, 2 * half2):
        l2y[i] = jnp.zeros((wide2, hz), F32)
    high, low = halves(jnp.concatenate([l2y[0:half2], l2y[half2 : 2 * half2]], axis=2).reshape(half2 * wide2, 2 * hz))
    l2p[...] = (dot(high, rz2[...]) + dot(low, rz2[...])).reshape(l2p.shape)
    pl.semaphore_wait(barrier, len(peers))
    lines = both([
        remote(l2p, seen2.at[0], 1, 0),
        remote(l2p, seen2.at[1], -1, 0),
        remote(l2p, seen2.at[2], 2, 0),
        remote(l2p, seen2.at[3], -2, 0),
    ])
    def edge_at(ref, d, i):
        return ref.at[d, i // 4, 2 * (i % 4) : 2 * (i % 4) + 2]

    first1 = (rows1 - margin - 1, 0)
    rim = []
    for d, dx in ((0, 1), (1, -1)):
        rim.append(remote(l1w.at[first1[d] : first1[d] + margin + 1, 0:hy], (low1, high1)[d], dx, 0))
        rim[-1].start()
    for i in range(margin + 1):
        for d in range(2):
            edge_at(edge, d, i)[...] = l1w[first1[d] + i, hy : hy + 2]
    rim += both([remote(edge.at[d], edge_in.at[d], dx, 0) for d, dx in ((0, 1), (1, -1))])
    g1 = bx // per
    steps = near_steps(radius)
    side = both([
        remote(fine.at[x0:x1, by - 8 : by], fine.at[x0:x1, by : by + 8], 0, 1),
        remote(fine.at[x0:x1, 0:8], fine.at[x0:x1, by + 8 : by + 16], 0, -1),
    ])
    for i in range(bx):
        g, r = i // per, extra * (i % per)
        ext[0, g, r : r + extra] = fine[x0 + i, by - radius : by - 8]
        ext[1, g, r : r + extra] = fine[x0 + i, 8:radius]

    side += both([
        remote(ext.at[0, 0:g1], got.at[0, 0:g1], 0, 1),
        remote(ext.at[1, 0:g1], got.at[1, 0:g1], 0, -1),
    ])
    def pick(first, second):
        return even * first + odd * second

    def span(start, size):
        return pl.ds(start, size)

    near = [
        both([remote(fine.at[span(pick(x1 - b, x0 + a), b - a), 0:by], fine.at[span(pick(x0 - b, x1 + a), b - a), 0:by], even - odd, 0)])
        for a, b in steps
    ]
    places2 = []
    for k in range(wy):
        at = wide2 * k
        places2 += [(at, ey * k - at), (at + ey + 2, ey * k - 3 - ey - at), (at + ey + 3, 1000)]
    y_table(ty2, 2, wide2, wy * wide2, low_y * ey + 1 + radius, wy * ey if ny <= 2 * reach + 1 else 0, places2)
    z_table(tz2, 2, ez)
    y_table(ty0, 0, by, by + 24, radius, 0, [(by, -by - 8), (by + 8, -8), (by + 16, -by - 16 - radius), (by + 16 + extra, -8 - extra), (by + 16 + 2 * extra, 1000)])
    low, high = wide1 + 16, wide1 + 16 + tip
    y_table(ty1, 1, wide1, wide1 + 16 + 2 * tip, radius + 1, 0, [
        (hy + 1, -hy - 2), (hy + 2, 1000), (wide1, -8 - wide1), (wide1 + 8, hy - wide1 - 8), (low, -margin - low),
        (low + tip - 1, -low - tip + 1), (high, hy + 8 - high), (high + tip - 1, hy - high - tip),
    ])
    z_table(tz0, 0, bz)
    spare = jnp.zeros((8 - 2 * extra, bz), F32)

    def unpack(rows, first):
        for n, i in enumerate(rows):
            g, r = first + n // per, extra * (n % per)
            fine[i, by + 16 : by + 16 + extra] = got[0, g, r : r + extra]
            fine[i, by + 16 + extra : by + 16 + 2 * extra] = got[1, g, r : r + extra]
            fine[i, by + 16 + 2 * extra : by + 24] = spare

    z_table(tz1, 1, hz)

    arrive(lines)
    home = radius
    pairs = cols2.shape[1]
    whole = [None] * (2 * pairs)
    for first, source in ((home, l2p), (home - ex, seen2.at[0]), (home + ex, seen2.at[1]), (home - 2 * ex, seen2.at[2]), (home + 2 * ex, seen2.at[3])):
        for r in range(rows2):
            if 0 <= first + r < rows2 + 2 * radius:
                piece = source[r % half2][:, (r // half2) * ez : (r // half2 + 1) * ez]
                whole[first + r] = piece if whole[first + r] is None else whole[first + r] + piece
    for j in range(pairs):
        top[j] = jnp.concatenate([jnp.zeros((wide2, ez), F32) if v is None else v for v in (whole[j], whole[j + pairs])], axis=1)
    if ny == 4:
        turn = 1 - 2 * lax.rem(me_y, 2)
        fan = both([remote(top, cols2.at[3], 0, 2), remote(top, cols2.at[1 - turn], 0, turn)])
    else:
        fan = both([remote(top, cols2.at[k], 0, -(low_y + k)) for k in range(wy) if low_y + k])
    cols2[-low_y] = top[...]
    def correlate_y(ref, source, table, rows, step, first=0):
        width = table.shape[0] // terms

        def one(i):
            i = i + first
            value = dot(table[...], stacked3(source[i]))
            for member in range(terms):
                ref[member, i] = value[member * width : (member + 1) * width]

        repeat(rows, step, one)

    def correlate_x(ref, source, level, rows, first, step, start=0):
        def one(i):
            i = i + start
            for member in range(terms):
                total = None
                for position in range(count):
                    piece = source[member, i + first + position] * tap(level, member, position)
                    total = piece if total is None else total + piece
                high, low = halves(total)
                at = slice(member * total.shape[1], (member + 1) * total.shape[1])
                ref[0, i, :, at] = high
                ref[1, i, :, at] = low

        repeat(rows, step, one)

    mid[:, hy:wide1] = jnp.zeros((mid.shape[0], wide1 - hy, hz), F32)
    mid[margin + 1 : margin + hx - 1, 0:wide1] = l1w[2:hx]
    arrive(rim)
    mid[0 : margin + 1, 0:hy] = low1[...]
    mid[margin + hx - 1 : margin + hx + margin, 0:hy] = high1[...]
    for i in range(margin + 1):
        for d, at in ((0, 0), (1, margin + hx - 1)):
            mid[at + i, hy : hy + 2] = edge_at(edge_in, d, i)[...]
    for i, j in ((margin - 1, 0), (margin, 1), (margin + hx - 1, hx), (margin + hx, hx + 1)):
        mid[i, 0:wide1] += l1w[j]
    rim2 = both([
        remote(mid.at[:, hy - 8 : hy], mid.at[:, wide1 : wide1 + 8], 0, 1),
        remote(mid.at[:, 0:8], mid.at[:, wide1 + 8 : wide1 + 16], 0, -1),
    ])
    for i in range(mid.shape[0]):
        g, r = i // tip_per, tip * (i % tip_per)
        for d, (a, b) in enumerate(((hy - margin, hy - 8), (8, margin))):
            tips[d, g, r : r + tip - 1] = mid[i, a:b]
            tips[d, g, r + tip - 1 : r + tip] = mid[i, hy + d : hy + d + 1]
    rim2 += both([remote(tips.at[d], tips_in.at[d], 0, dy) for d, dy in ((0, 1), (1, -1))])
    far = [
        both([remote(fine.at[span(pick(x0 + a, x1 - b), b - a), 0:by], fine.at[span(pick(x1 + a, x0 - b), b - a), 0:by], odd - even, 0)])
        for a, b in steps
    ]

    def correlate_z(ref, table, rows, count):
        size = count * ref.shape[2]
        high = ref[0, rows].reshape(size, ref.shape[3])
        low = ref[1, rows].reshape(size, ref.shape[3])
        return dot(high, table[0]) + dot(low, table[0]) + dot(high, table[1])

    def prolong_x(source, j, first):
        at = j - 2 * first
        if j % 2 == 0:
            c = (j // 2) - first
            return source[c - 1] * 0.125 + source[c] * 0.75 + source[c + 1] * 0.125
        c = (j - 1) // 2 - first
        return source[c] * 0.5 + source[c + 1] * 0.5

    arrive(side)
    unpack(range(x0, x1), 0)
    correlate_y(y0, fine, ty0, bx, 4, x0)
    correlate_x(s0, y0, 0, bx - 2 * radius, 0, 1, radius)
    if ny == 4:
        arrive(fan[:1])
        fan = both([remote(cols2.at[3], cols2.at[1 + turn], 0, turn)]) + fan[1:] + fan[:1]
    for e in range(radius):
        for edge_of, i in ((0, e), (1, bx - 1 - e)):
            for member in range(terms):
                total = None
                for position in range(count):
                    if x0 <= i + position < x1:
                        piece = y0[member, i + position] * tap(0, member, position)
                        total = piece if total is None else total + piece
                part[edge_of, e, member] = total

    def add_halo(edge_of, a, b):
        def choose(first, last):
            return (1 - edge_of) * first + edge_of * last

        for e in range(radius - a):
            i = choose(e, bx - 1 - e)
            for member in range(terms):
                total = part[edge_of, e, member]
                for k in range(a, min(b, radius - e)):
                    weight = tap(0, member, choose(radius - 1 - k - e, radius + 1 + k + e))
                    total = total + y0[member, choose(x0 - 1 - k, x1 + k)] * weight
                if radius - e > b:
                    part[edge_of, e, member] = total
                else:
                    high, low = halves(total)
                    s0[0, i, :, member * bz : (member + 1) * bz] = high
                    s0[1, i, :, member * bz : (member + 1) * bz] = low

    def pack(start, size, group):
        for n in range(size):
            g, r = group + n // per, extra * (n % per)
            ext[0, g, r : r + extra] = fine[start + n, by - radius : by - 8, :]
            ext[1, g, r : r + extra] = fine[start + n, 8:radius, :]
        rows, groups = span(start, size), slice(group, group - (-size // per))
        return both([
            remote(fine.at[rows, by - 8 : by], fine.at[rows, by : by + 8], 0, 1),
            remote(fine.at[rows, 0:8], fine.at[rows, by + 8 : by + 16], 0, -1),
            remote(ext.at[0, groups], got.at[0, groups], 0, 1),
            remote(ext.at[1, groups], got.at[1, groups], 0, -1),
        ])

    parts = [(a, b, pick(x0 - b, x1 + a), pick(radius - b, bx - radius + a), odd) for a, b in steps] + [
        (a, b, pick(x1 + a, x0 - b), pick(bx - radius + a, radius - b), even) for a, b in steps
    ]
    groups = [g1]
    for a, b, _, _, _ in parts:
        groups.append(groups[-1] + -(-(b - a) // per))
    corners = []

    def relay(copies):
        n = len(corners)
        a, b, halo, _, _ = parts[n]
        arrive(copies)
        corners.append(pack(halo, b - a, groups[n]))

    arrive(fan[:2] if ny == 4 else fan)
    for j in range(pairs):
        value = dot(ty2[...], stacked3(jnp.concatenate([cols2[k, j] for k in range(wy)], axis=0)))
        for member in range(terms):
            y2[member, j] = value[member * wide2 : (member + 1) * wide2, 0:ez]
            y2[member, j + pairs] = value[member * wide2 : (member + 1) * wide2, ez : 2 * ez]
    correlate_x(s2, y2, 2, rows2, 0, 1)
    tx[...] = correlate_z(s2, tz2, slice(0, rows2), rows2).reshape(tx.shape)
    for j in range(hx + 2):
        ty[j] = dot(uy2[...], stacked2(prolong_x(tx, j - 1, -1)))
    high, low = halves(ty[...].reshape((hx + 2) * ty.shape[1], ez))
    lifted = dot(high, uz2[...]) + dot(low, uz2[...])

    md[...] = lifted.reshape(md.shape)
    relay(far[0])
    arrive(rim2)
    for i in range(mid.shape[0]):
        g, r = i // tip_per, tip * (i % tip_per)
        for d in range(2):
            mid[i, wide1 + 16 + tip * d : wide1 + 16 + tip * (d + 1)] = tips_in[d, g, r : r + tip]
    correlate_y(y1, mid, ty1, hx + 2 * margin, (hx + 2 * margin) // 2)
    early = (hx + 2) // 2
    correlate_x(s1, y1, 1, early, 0, 1)
    relay(far[1])
    correlate_x(s1, y1, 1, hx + 2 - early, 0, 1, early)
    md[...] += correlate_z(s1, tz1, slice(0, hx + 2), hx + 2).reshape(md.shape)
    for j in range(bx):
        high, low = halves(dot(uy1[...], stacked2(prolong_x(md, j, -1))))
        my[0, j] = high
        my[1, j] = low

    def finish(start, size):
        rows = span(start, size)
        high = my[0, rows].reshape(size * by, hz)
        low = my[1, rows].reshape(size * by, hz)
        total = correlate_z(s0, tz0, rows, size) + dot(high, uz1[...]) + dot(low, uz1[...])
        out[rows] = total.reshape(size, by, bz)

    relay(near[0])
    finish(radius, bx - 2 * radius)
    for n, (a, b, halo, target, edge_of) in enumerate(parts):
        arrive(corners[n])
        unpack([halo + k for k in range(b - a)], groups[n])
        correlate_y(y0, fine, ty0, b - a, (b - a) // 2, halo)
        add_halo(edge_of, a, b)
        if n == 0:
            relay(near[1])
        finish(target, b - a)
    for copy in fan + rim + side + lines + sum(near + far, []) + rim2 + sum(corners, []):
        copy.wait_send()


def near_steps(radius):
    first = min(radius, radius // 2 + radius // 2 % 2)
    return [(0, first), (first, radius)]


def body(charges, kernel_taps):
    nx, ny = lax.axis_size("gx"), lax.axis_size("gy")
    levels, terms, count = kernel_taps.shape
    radius = count // 2
    margin = radius + 1
    bx, by, bz = charges.shape
    hx, hy, hz = bx // 2, by // 2, bz // 2
    ex, ey, ez = bx // 4, by // 4, bz // 4
    wy = min(ny, 5)
    wide1 = hy + 8
    wide2 = ey + 8
    tables = [(wide1, 2 * by), (bz, hz), (wide2, 2 * wide1), (2 * hz, 2 * ez), (wide1, 2 * wide2), (ez, hz), (by, 2 * wide1), (hz, bz)]
    rows1, rows2 = hx + 2, ex + 3
    half2, pairs = (rows2 + 1) // 2, (rows2 + 2 * radius + 1) // 2
    extra = radius - 8
    tip = margin - 7
    packed = bx * extra // 8 + sum(-(-(b - a) * extra // 8) for a, b in 2 * near_steps(radius))
    scratch = [pltpu.SMEM(kernel_taps.shape, F32)] + [pltpu.VMEM(shape, BF16) for shape in tables] + [
        pltpu.VMEM(shape, dtype)
        for shape, dtype in (
            ((bx + 2 * radius, by + 24, bz), F32),
            ((hx + 2 * margin, wide1 + 16 + 2 * tip, hz), F32),
            ((2, packed, 8, bz), F32),
            ((2, packed, 8, bz), F32),
            ((2, -(-(hx + 2 * margin) // (8 // tip)), 8, hz), F32),
            ((2, -(-(hx + 2 * margin) // (8 // tip)), 8, hz), F32),
            ((margin + 1, hy, hz), F32),
            ((margin + 1, hy, hz), F32),
            ((half2, wide2, 2 * ez), F32),
            ((wy, pairs, wide2, 2 * ez), F32),
            ((4, half2, wide2, 2 * ez), F32),
            ((pairs, wide2, 2 * ez), F32),
            ((terms * by, 3 * (by + 24)), BF16),
            ((terms * wide1, 3 * (wide1 + 16 + 2 * tip)), BF16),
            ((terms * wide2, 3 * wy * wide2), BF16),
            ((2, terms * bz, bz), BF16),
            ((2, terms * hz, hz), BF16),
            ((2, terms * ez, ez), BF16),
            ((terms, bx + 2 * radius, by, bz), F32),
            ((2, bx, by, terms * bz), BF16),
            ((terms, hx + 2 * margin, wide1, hz), F32),
            ((2, hx + 2, wide1, terms * hz), BF16),
            ((terms, 2 * pairs, wide2, ez), F32),
            ((2, rows2, wide2, terms * ez), BF16),
            ((rows1, wide1, bz), F32),
            ((rows1, wide1, hz), F32),
            ((2 * half2, wide2, hz), F32),
            ((rows2, wide2, ez), F32),
            ((hx + 2, wide1, ez), F32),
            ((hx + 2, wide1, hz), F32),
            ((2, bx, by, hz), BF16),
            ((2, -(-2 * (margin + 1) // 8), 8, hz), F32),
            ((2, -(-2 * (margin + 1) // 8), 8, hz), F32),
            ((2, radius, terms, by, bz), F32),
        )
    ] + [
        pltpu.SemaphoreType.DMA((40,)),
        pltpu.SemaphoreType.DMA((40,)),
        pltpu.SemaphoreType.DMA((2,)),
    ]
    result = pl.pallas_call(
        functools.partial(kernel, nx, ny, radius, terms),
        out_shape=jax.ShapeDtypeStruct(charges.shape, F32),
        in_specs=[pl.BlockSpec(memory_space=pltpu.HBM)] * 2,
        out_specs=pl.BlockSpec(memory_space=pltpu.VMEM),
        scratch_shapes=scratch,
        compiler_params=pltpu.CompilerParams(
            collective_id=0, has_side_effects=True, vmem_limit_bytes=211 * 2**18
        ),
    )(kernel_taps, charges)
    return result


def solution(mesh):
    return jax.shard_map(
        body,
        mesh=mesh,
        in_specs=(P("gx", "gy", None), P()),
        out_specs=P("gx", "gy", None),
        check_vma=False,
    )
```

```python
import functools

import jax
import jax.numpy as jnp
from jax import lax
from jax.experimental import pallas as pl
from jax.experimental.pallas import tpu as pltpu
from jax.sharding import PartitionSpec as P

SPLINE = (0.125, 0.5, 0.75, 0.5, 0.125)
F32, BF16 = jnp.float32, jnp.bfloat16
MESH = pl.DeviceIdType.MESH


def halves(value):
    high = value.astype(BF16)
    return high, (value - high.astype(F32)).astype(BF16)


def dot(left, right):
    return jnp.dot(left, right, preferred_element_type=F32)


def stacked2(value):
    high, low = halves(value)
    return jnp.concatenate([high, low], axis=0)


def stacked3(value):
    high, low = halves(value)
    return jnp.concatenate([high, low, high], axis=0)


def repeat(count, step, body):
    def trip(i, carry):
        for k in range(step):
            body(i * step + k)
        return carry

    assert count % step == 0
    lax.fori_loop(0, count // step, trip, 0)


def kernel(nx, ny, radius, terms, *refs):
    given, out, held, refs = refs[:2], refs[2], refs[3:12], refs[12:]
    taps, ry1, rz1, ry2, rz2, uy2, uz2, uy1, uz1 = held
    (fine, mid, ext, got, tips, tips_in, low1, high1, l2p, cols2, seen2, top,
           ty0, ty1, ty2, tz0, tz1, tz2, y0, s0, y1, s1, y2, s2, r1, l1w, l2y, tx, ty, md, my,
     edge, edge_in, part, send, recv, load) = refs
    bx, by, bz = given[1].shape
    x0, x1 = radius, radius + bx
    hx, hy, hz = bx // 2, by // 2, bz // 2
    ex, ey, ez = bx // 4, by // 4, bz // 4
    count = 2 * radius + 1
    margin = radius + 1
    me_x, me_y = lax.axis_index("gx"), lax.axis_index("gy")
    reach = 2
    odd = lax.rem(me_x, 2) if nx % 2 == 0 else 0
    even = 1 - odd
    wy = min(ny, 2 * reach + 1)
    low_y = -((wy - 1) // 2)

    def device(dx, dy):
        return {"gx": lax.rem(me_x + dx + nx, nx), "gy": lax.rem(me_y + dy + ny, ny)}

    peers = {}
    for dx, dy in [(-1, 0), (1, 0), (0, -1), (0, 1), (-2, 0), (2, 0)] + [
        (0, -(low_y + k)) for k in range(wy)
    ]:
        if dx % nx or dy % ny:
            peers[(dx % nx, dy % ny)] = (dx, dy)
    barrier = pltpu.get_barrier_semaphore()
    for dx, dy in peers.values():
        pl.semaphore_signal(barrier, inc=1, device_id=device(dx, dy), device_id_type=MESH)

    fetched = [
        pltpu.make_async_copy(source, target, load.at[n])
        for n, (source, target) in enumerate(zip(given, [taps, fine.at[x0:x1, 0:by]]))
    ]
    for copy in fetched:
        copy.start()

    def tap(level, member, position):
        return taps[level, member, position]

    def band(level, member, rows, cols, first, cycle, places):
        column = lax.broadcasted_iota(jnp.int32, (rows, cols), 1)
        place = column
        for start, shift in places:
            place = jnp.where(column >= start, column + shift, place)
        offsets = place - lax.broadcasted_iota(jnp.int32, (rows, cols), 0) + first
        if cycle:
            offsets = jnp.where(offsets < 0, offsets + cycle, offsets)
            offsets = jnp.where(offsets >= cycle, offsets - cycle, offsets)
        table = jnp.zeros((rows, cols), F32)
        for position in range(count):
            table = jnp.where(offsets == position, tap(level, member, position), table)
        return table

    def y_table(ref, level, rows, cols, first, cycle, places):
        for member in range(terms):
            high, low = halves(band(level, member, rows, cols, first, cycle, places))
            at = slice(member * rows, (member + 1) * rows)
            ref[at, 0:cols] = high
            ref[at, cols : 2 * cols] = high
            ref[at, 2 * cols : 3 * cols] = low

    def z_table(ref, level, n):
        def rows_of(i):
            start = pl.multiple_of(i * 16, 16)
            offsets = (
                lax.broadcasted_iota(jnp.int32, (16, n), 0)
                + start
                - lax.broadcasted_iota(jnp.int32, (16, n), 1)
                + radius
            )
            offsets = jnp.where(offsets < 0, offsets + n, offsets)
            offsets = jnp.where(offsets >= n, offsets - n, offsets)
            for member in range(terms):
                table = jnp.zeros((16, n), F32)
                for position in range(count):
                    table = jnp.where(offsets == position, tap(level, member, position), table)
                high, low = halves(table)
                ref[0, pl.ds(pl.multiple_of(member * n + start, 16), 16), :] = high
                ref[1, pl.ds(pl.multiple_of(member * n + start, 16), 16), :] = low

        repeat(n // 16, 1, rows_of)

    sem = [0]

    def remote(source, target, dx, dy):
        index = sem[0]
        sem[0] += 1
        return pltpu.make_async_remote_copy(
            src_ref=source, dst_ref=target, send_sem=send.at[index], recv_sem=recv.at[index],
            device_id=device(dx, dy), device_id_type=MESH,
        )

    def both(copies):
        for copy in copies:
            copy.start()
        return copies

    def arrive(copies):
        for copy in copies:
            copy.wait_recv()

    extra = radius - 8
    per = 8 // extra
    tip = margin - 7
    tip_per = 8 // tip
    def weighted(source, i, low, high):
        total = None
        for k in range(-2, 3):
            if low <= 2 * i + k < high:
                piece = source(2 * i + k) * SPLINE[k + 2]
                total = piece if total is None else total + piece
        return total

    def places(shape, axis):
        return lax.broadcasted_iota(jnp.int32, shape, axis)

    def spline_table(ref, offset, valid):
        distance = jnp.abs(offset)
        value = jnp.where(distance == 0, SPLINE[2], jnp.where(distance == 1, SPLINE[1], jnp.where(distance == 2, SPLINE[0], 0.0)))
        ref[...] = jnp.where(valid, value, 0.0).astype(BF16)

    def folded(index, width):
        return jnp.where(index >= width, index - width, index)

    def along_z(ref, fine_axis, n, blocks):
        rows, cols = places(ref.shape, fine_axis), places(ref.shape, 1 - fine_axis)
        same = (rows >= n) == (cols >= n // 2) if blocks == 2 else rows >= 0
        offset = folded(rows, n) - 2 * folded(cols, n // 2) if blocks == 2 else rows - 2 * cols
        offset = jnp.where(offset > n // 2, offset - n, jnp.where(offset < -(n // 2), offset + n, offset))
        spline_table(ref, offset, same)

    a, b = places(ry1.shape, 0), folded(places(ry1.shape, 1), by)
    spline_table(ry1, b - 2 * jnp.where(a == hy + 1, -1, a), a <= hy + 1)
    a, b = places(ry2.shape, 0), folded(places(ry2.shape, 1), ry1.shape[0])
    spline_table(ry2, jnp.where(b == hy + 1, -1, b) - 2 * jnp.where(a == ey + 2, -1, a), (a <= ey + 2) & (b <= hy + 1))
    a, b = places(uy2.shape, 0), folded(places(uy2.shape, 1), ry2.shape[0])
    spline_table(uy2, a + 1 - 2 * b, (a < hy + 2) & (b < ey + 3))
    a, b = places(uy1.shape, 0), folded(places(uy1.shape, 1), ry1.shape[0])
    spline_table(uy1, a + 2 - 2 * b, b < hy + 2)
    along_z(rz1, 0, bz, 1)
    along_z(uz1, 1, bz, 1)
    along_z(rz2, 0, hz, 2)
    along_z(uz2, 1, hz, 1)
    for copy in fetched:
        copy.wait()
    rows1, rows2 = hx + 2, ex + 3
    half2 = l2p.shape[0]
    wide1, wide2 = ry1.shape[0], ry2.shape[0]
    for i in range(rows1):
        r1[i] = dot(ry1[...], stacked2(weighted(lambda f: fine[x0 + f, 0:by], i - 1, 0, bx)))
    high, low = halves(r1[...].reshape(rows1 * wide1, bz))
    l1w[...] = (dot(high, rz1[...]) + dot(low, rz1[...])).reshape(rows1, wide1, hz)
    for i in range(rows2):
        l2y[i] = dot(ry2[...], stacked2(weighted(lambda f: l1w[f + 1], i - 1, -1, hx + 1)))
    for i in range(rows2, 2 * half2):
        l2y[i] = jnp.zeros((wide2, hz), F32)
    high, low = halves(jnp.concatenate([l2y[0:half2], l2y[half2 : 2 * half2]], axis=2).reshape(half2 * wide2, 2 * hz))
    l2p[...] = (dot(high, rz2[...]) + dot(low, rz2[...])).reshape(l2p.shape)
    pl.semaphore_wait(barrier, len(peers))
    lines = both([
        remote(l2p, seen2.at[0], 1, 0),
        remote(l2p, seen2.at[1], -1, 0),
        remote(l2p, seen2.at[2], 2, 0),
        remote(l2p, seen2.at[3], -2, 0),
    ])
    def edge_at(ref, d, i):
        return ref.at[d, i // 4, 2 * (i % 4) : 2 * (i % 4) + 2]

    first1 = (rows1 - margin - 1, 0)
    rim = []
    for d, dx in ((0, 1), (1, -1)):
        rim.append(remote(l1w.at[first1[d] : first1[d] + margin + 1, 0:hy], (low1, high1)[d], dx, 0))
        rim[-1].start()
    for i in range(margin + 1):
        for d in range(2):
            edge_at(edge, d, i)[...] = l1w[first1[d] + i, hy : hy + 2]
    rim += both([remote(edge.at[d], edge_in.at[d], dx, 0) for d, dx in ((0, 1), (1, -1))])
    g1 = bx // per
    steps = near_steps(radius)
    side = both([
        remote(fine.at[x0:x1, by - 8 : by], fine.at[x0:x1, by : by + 8], 0, 1),
        remote(fine.at[x0:x1, 0:8], fine.at[x0:x1, by + 8 : by + 16], 0, -1),
    ])
    for i in range(bx):
        g, r = i // per, extra * (i % per)
        ext[0, g, r : r + extra] = fine[x0 + i, by - radius : by - 8]
        ext[1, g, r : r + extra] = fine[x0 + i, 8:radius]

    side += both([
        remote(ext.at[0, 0:g1], got.at[0, 0:g1], 0, 1),
        remote(ext.at[1, 0:g1], got.at[1, 0:g1], 0, -1),
    ])
    def pick(first, second):
        return even * first + odd * second

    def span(start, size):
        return pl.ds(start, size)

    near = [
        both([remote(fine.at[span(pick(x1 - b, x0 + a), b - a), 0:by], fine.at[span(pick(x0 - b, x1 + a), b - a), 0:by], even - odd, 0)])
        for a, b in steps
    ]
    places2 = []
    for k in range(wy):
        at = wide2 * k
        places2 += [(at, ey * k - at), (at + ey + 2, ey * k - 3 - ey - at), (at + ey + 3, 1000)]
    y_table(ty2, 2, wide2, wy * wide2, low_y * ey + 1 + radius, wy * ey if ny <= 2 * reach + 1 else 0, places2)
    z_table(tz2, 2, ez)
    y_table(ty0, 0, by, by + 24, radius, 0, [(by, -by - 8), (by + 8, -8), (by + 16, -by - 16 - radius), (by + 16 + extra, -8 - extra), (by + 16 + 2 * extra, 1000)])
    low, high = wide1 + 16, wide1 + 16 + tip
    y_table(ty1, 1, wide1, wide1 + 16 + 2 * tip, radius + 1, 0, [
        (hy + 1, -hy - 2), (hy + 2, 1000), (wide1, -8 - wide1), (wide1 + 8, hy - wide1 - 8), (low, -margin - low),
        (low + tip - 1, -low - tip + 1), (high, hy + 8 - high), (high + tip - 1, hy - high - tip),
    ])
    z_table(tz0, 0, bz)
    spare = jnp.zeros((8 - 2 * extra, bz), F32)

    def unpack(rows, first):
        for n, i in enumerate(rows):
            g, r = first + n // per, extra * (n % per)
            fine[i, by + 16 : by + 16 + extra] = got[0, g, r : r + extra]
            fine[i, by + 16 + extra : by + 16 + 2 * extra] = got[1, g, r : r + extra]
            fine[i, by + 16 + 2 * extra : by + 24] = spare

    z_table(tz1, 1, hz)

    arrive(lines)
    home = radius
    pairs = cols2.shape[1]
    whole = [None] * (2 * pairs)
    for first, source in ((home, l2p), (home - ex, seen2.at[0]), (home + ex, seen2.at[1]), (home - 2 * ex, seen2.at[2]), (home + 2 * ex, seen2.at[3])):
        for r in range(rows2):
            if 0 <= first + r < rows2 + 2 * radius:
                piece = source[r % half2][:, (r // half2) * ez : (r // half2 + 1) * ez]
                whole[first + r] = piece if whole[first + r] is None else whole[first + r] + piece
    for j in range(pairs):
        top[j] = jnp.concatenate([jnp.zeros((wide2, ez), F32) if v is None else v for v in (whole[j], whole[j + pairs])], axis=1)
    if ny == 4:
        turn = 1 - 2 * lax.rem(me_y, 2)
        fan = both([remote(top, cols2.at[3], 0, 2), remote(top, cols2.at[1 - turn], 0, turn)])
    else:
        fan = both([remote(top, cols2.at[k], 0, -(low_y + k)) for k in range(wy) if low_y + k])
    cols2[-low_y] = top[...]
    def correlate_y(ref, source, table, rows, step, first=0):
        width = table.shape[0] // terms

        def one(i):
            i = i + first
            value = dot(table[...], stacked3(source[i]))
            for member in range(terms):
                ref[member, i] = value[member * width : (member + 1) * width]

        repeat(rows, step, one)

    def correlate_x(ref, source, level, rows, first, step, start=0):
        def one(i):
            i = i + start
            for member in range(terms):
                total = None
                for position in range(count):
                    piece = source[member, i + first + position] * tap(level, member, position)
                    total = piece if total is None else total + piece
                high, low = halves(total)
                at = slice(member * total.shape[1], (member + 1) * total.shape[1])
                ref[0, i, :, at] = high
                ref[1, i, :, at] = low

        repeat(rows, step, one)

    mid[:, hy:wide1] = jnp.zeros((mid.shape[0], wide1 - hy, hz), F32)
    mid[margin + 1 : margin + hx - 1, 0:wide1] = l1w[2:hx]
    arrive(rim)
    mid[0 : margin + 1, 0:hy] = low1[...]
    mid[margin + hx - 1 : margin + hx + margin, 0:hy] = high1[...]
    for i in range(margin + 1):
        for d, at in ((0, 0), (1, margin + hx - 1)):
            mid[at + i, hy : hy + 2] = edge_at(edge_in, d, i)[...]
    for i, j in ((margin - 1, 0), (margin, 1), (margin + hx - 1, hx), (margin + hx, hx + 1)):
        mid[i, 0:wide1] += l1w[j]
    rim2 = both([
        remote(mid.at[:, hy - 8 : hy], mid.at[:, wide1 : wide1 + 8], 0, 1),
        remote(mid.at[:, 0:8], mid.at[:, wide1 + 8 : wide1 + 16], 0, -1),
    ])
    for i in range(mid.shape[0]):
        g, r = i // tip_per, tip * (i % tip_per)
        for d, (a, b) in enumerate(((hy - margin, hy - 8), (8, margin))):
            tips[d, g, r : r + tip - 1] = mid[i, a:b]
            tips[d, g, r + tip - 1 : r + tip] = mid[i, hy + d : hy + d + 1]
    rim2 += both([remote(tips.at[d], tips_in.at[d], 0, dy) for d, dy in ((0, 1), (1, -1))])
    far = [
        both([remote(fine.at[span(pick(x0 + a, x1 - b), b - a), 0:by], fine.at[span(pick(x1 + a, x0 - b), b - a), 0:by], odd - even, 0)])
        for a, b in steps
    ]

    def correlate_z(ref, table, rows, count):
        size = count * ref.shape[2]
        high = ref[0, rows].reshape(size, ref.shape[3])
        low = ref[1, rows].reshape(size, ref.shape[3])
        return dot(high, table[0]) + dot(low, table[0]) + dot(high, table[1])

    def prolong_x(source, j, first):
        at = j - 2 * first
        if j % 2 == 0:
            c = (j // 2) - first
            return source[c - 1] * 0.125 + source[c] * 0.75 + source[c + 1] * 0.125
        c = (j - 1) // 2 - first
        return source[c] * 0.5 + source[c + 1] * 0.5

    arrive(side)
    unpack(range(x0, x1), 0)
    correlate_y(y0, fine, ty0, bx, 4, x0)
    correlate_x(s0, y0, 0, bx - 2 * radius, 0, 1, radius)
    if ny == 4:
        arrive(fan[:1])
        fan = both([remote(cols2.at[3], cols2.at[1 + turn], 0, turn)]) + fan[1:] + fan[:1]
    for e in range(radius):
        for edge_of, i in ((0, e), (1, bx - 1 - e)):
            for member in range(terms):
                total = None
                for position in range(count):
                    if x0 <= i + position < x1:
                        piece = y0[member, i + position] * tap(0, member, position)
                        total = piece if total is None else total + piece
                part[edge_of, e, member] = total

    def add_halo(edge_of, a, b):
        def choose(first, last):
            return (1 - edge_of) * first + edge_of * last

        for e in range(radius - a):
            i = choose(e, bx - 1 - e)
            for member in range(terms):
                total = part[edge_of, e, member]
                for k in range(a, min(b, radius - e)):
                    weight = tap(0, member, choose(radius - 1 - k - e, radius + 1 + k + e))
                    total = total + y0[member, choose(x0 - 1 - k, x1 + k)] * weight
                if radius - e > b:
                    part[edge_of, e, member] = total
                else:
                    high, low = halves(total)
                    s0[0, i, :, member * bz : (member + 1) * bz] = high
                    s0[1, i, :, member * bz : (member + 1) * bz] = low

    def pack(start, size, group):
        for n in range(size):
            g, r = group + n // per, extra * (n % per)
            ext[0, g, r : r + extra] = fine[start + n, by - radius : by - 8, :]
            ext[1, g, r : r + extra] = fine[start + n, 8:radius, :]
        rows, groups = span(start, size), slice(group, group - (-size // per))
        return both([
            remote(fine.at[rows, by - 8 : by], fine.at[rows, by : by + 8], 0, 1),
            remote(fine.at[rows, 0:8], fine.at[rows, by + 8 : by + 16], 0, -1),
            remote(ext.at[0, groups], got.at[0, groups], 0, 1),
            remote(ext.at[1, groups], got.at[1, groups], 0, -1),
        ])

    parts = [(a, b, pick(x0 - b, x1 + a), pick(radius - b, bx - radius + a), odd) for a, b in steps] + [
        (a, b, pick(x1 + a, x0 - b), pick(bx - radius + a, radius - b), even) for a, b in steps
    ]
    groups = [g1]
    for a, b, _, _, _ in parts:
        groups.append(groups[-1] + -(-(b - a) // per))
    corners = []

    def relay(copies):
        n = len(corners)
        a, b, halo, _, _ = parts[n]
        arrive(copies)
        corners.append(pack(halo, b - a, groups[n]))

    arrive(fan[:2] if ny == 4 else fan)
    for j in range(pairs):
        value = dot(ty2[...], stacked3(jnp.concatenate([cols2[k, j] for k in range(wy)], axis=0)))
        for member in range(terms):
            y2[member, j] = value[member * wide2 : (member + 1) * wide2, 0:ez]
            y2[member, j + pairs] = value[member * wide2 : (member + 1) * wide2, ez : 2 * ez]
    correlate_x(s2, y2, 2, rows2, 0, rows2)
    tx[...] = correlate_z(s2, tz2, slice(0, rows2), rows2).reshape(tx.shape)
    for j in range(hx + 2):
        ty[j] = dot(uy2[...], stacked2(prolong_x(tx, j - 1, -1)))
    high, low = halves(ty[...].reshape((hx + 2) * ty.shape[1], ez))
    lifted = dot(high, uz2[...]) + dot(low, uz2[...])

    md[...] = lifted.reshape(md.shape)
    relay(far[0])
    arrive(rim2)
    for i in range(mid.shape[0]):
        g, r = i // tip_per, tip * (i % tip_per)
        for d in range(2):
            mid[i, wide1 + 16 + tip * d : wide1 + 16 + tip * (d + 1)] = tips_in[d, g, r : r + tip]
    correlate_y(y1, mid, ty1, hx + 2 * margin, (hx + 2 * margin) // 2)
    early = (hx + 2) // 2
    correlate_x(s1, y1, 1, early, 0, 1)
    relay(far[1])
    correlate_x(s1, y1, 1, hx + 2 - early, 0, 1, early)
    md[...] += correlate_z(s1, tz1, slice(0, hx + 2), hx + 2).reshape(md.shape)
    for j in range(0, bx, 2):
        pair = jnp.concatenate([prolong_x(md, j, -1), prolong_x(md, j + 1, -1)], axis=1)
        high, low = halves(dot(uy1[...], stacked2(pair)))
        for k in range(2):
            my[0, j + k] = high[:, k * hz : (k + 1) * hz]
            my[1, j + k] = low[:, k * hz : (k + 1) * hz]

    def finish(start, size):
        rows = span(start, size)
        high = my[0, rows].reshape(size * by, hz)
        low = my[1, rows].reshape(size * by, hz)
        total = correlate_z(s0, tz0, rows, size) + dot(high, uz1[...]) + dot(low, uz1[...])
        out[rows] = total.reshape(size, by, bz)

    relay(near[0])
    finish(radius, bx - 2 * radius)
    for n, (a, b, halo, target, edge_of) in enumerate(parts):
        arrive(corners[n])
        unpack([halo + k for k in range(b - a)], groups[n])
        correlate_y(y0, fine, ty0, b - a, (b - a) // 2, halo)
        add_halo(edge_of, a, b)
        if n == 0:
            relay(near[1])
        finish(target, b - a)
    for copy in fan + rim + side + lines + sum(near + far, []) + rim2 + sum(corners, []):
        copy.wait_send()


def near_steps(radius):
    first = min(radius, radius // 2 + radius // 2 % 2)
    return [(0, first), (first, radius)]


def body(charges, kernel_taps):
    nx, ny = lax.axis_size("gx"), lax.axis_size("gy")
    levels, terms, count = kernel_taps.shape
    radius = count // 2
    margin = radius + 1
    bx, by, bz = charges.shape
    hx, hy, hz = bx // 2, by // 2, bz // 2
    ex, ey, ez = bx // 4, by // 4, bz // 4
    wy = min(ny, 5)
    wide1 = hy + 8
    wide2 = ey + 8
    tables = [(wide1, 2 * by), (bz, hz), (wide2, 2 * wide1), (2 * hz, 2 * ez), (wide1, 2 * wide2), (ez, hz), (by, 2 * wide1), (hz, bz)]
    rows1, rows2 = hx + 2, ex + 3
    half2, pairs = (rows2 + 1) // 2, (rows2 + 2 * radius + 1) // 2
    extra = radius - 8
    tip = margin - 7
    packed = bx * extra // 8 + sum(-(-(b - a) * extra // 8) for a, b in 2 * near_steps(radius))
    scratch = [pltpu.SMEM(kernel_taps.shape, F32)] + [pltpu.VMEM(shape, BF16) for shape in tables] + [
        pltpu.VMEM(shape, dtype)
        for shape, dtype in (
            ((bx + 2 * radius, by + 24, bz), F32),
            ((hx + 2 * margin, wide1 + 16 + 2 * tip, hz), F32),
            ((2, packed, 8, bz), F32),
            ((2, packed, 8, bz), F32),
            ((2, -(-(hx + 2 * margin) // (8 // tip)), 8, hz), F32),
            ((2, -(-(hx + 2 * margin) // (8 // tip)), 8, hz), F32),
            ((margin + 1, hy, hz), F32),
            ((margin + 1, hy, hz), F32),
            ((half2, wide2, 2 * ez), F32),
            ((wy, pairs, wide2, 2 * ez), F32),
            ((4, half2, wide2, 2 * ez), F32),
            ((pairs, wide2, 2 * ez), F32),
            ((terms * by, 3 * (by + 24)), BF16),
            ((terms * wide1, 3 * (wide1 + 16 + 2 * tip)), BF16),
            ((terms * wide2, 3 * wy * wide2), BF16),
            ((2, terms * bz, bz), BF16),
            ((2, terms * hz, hz), BF16),
            ((2, terms * ez, ez), BF16),
            ((terms, bx + 2 * radius, by, bz), F32),
            ((2, bx, by, terms * bz), BF16),
            ((terms, hx + 2 * margin, wide1, hz), F32),
            ((2, hx + 2, wide1, terms * hz), BF16),
            ((terms, 2 * pairs, wide2, ez), F32),
            ((2, rows2, wide2, terms * ez), BF16),
            ((rows1, wide1, bz), F32),
            ((rows1, wide1, hz), F32),
            ((2 * half2, wide2, hz), F32),
            ((rows2, wide2, ez), F32),
            ((hx + 2, wide1, ez), F32),
            ((hx + 2, wide1, hz), F32),
            ((2, bx, by, hz), BF16),
            ((2, -(-2 * (margin + 1) // 8), 8, hz), F32),
            ((2, -(-2 * (margin + 1) // 8), 8, hz), F32),
            ((2, radius, terms, by, bz), F32),
        )
    ] + [
        pltpu.SemaphoreType.DMA((40,)),
        pltpu.SemaphoreType.DMA((40,)),
        pltpu.SemaphoreType.DMA((2,)),
    ]
    result = pl.pallas_call(
        functools.partial(kernel, nx, ny, radius, terms),
        out_shape=jax.ShapeDtypeStruct(charges.shape, F32),
        in_specs=[pl.BlockSpec(memory_space=pltpu.HBM)] * 2,
        out_specs=pl.BlockSpec(memory_space=pltpu.VMEM),
        scratch_shapes=scratch,
        compiler_params=pltpu.CompilerParams(
            collective_id=0, has_side_effects=True, vmem_limit_bytes=211 * 2**18
        ),
    )(kernel_taps, charges)
    return result


def solution(mesh):
    return jax.shard_map(
        body,
        mesh=mesh,
        in_specs=(P("gx", "gy", None), P()),
        out_specs=P("gx", "gy", None),
        check_vma=False,
    )
```

```python
import functools

import jax
import jax.numpy as jnp
from jax import lax
from jax.experimental import pallas as pl
from jax.experimental.pallas import tpu as pltpu
from jax.sharding import PartitionSpec as P

SPLINE = (0.125, 0.5, 0.75, 0.5, 0.125)
F32, BF16 = jnp.float32, jnp.bfloat16
MESH = pl.DeviceIdType.MESH


def halves(value):
    high = value.astype(BF16)
    return high, (value - high.astype(F32)).astype(BF16)


def dot(left, right):
    return jnp.dot(left, right, preferred_element_type=F32)


def stacked2(value):
    high, low = halves(value)
    return jnp.concatenate([high, low], axis=0)


def stacked3(value):
    high, low = halves(value)
    return jnp.concatenate([high, low, high], axis=0)


def repeat(count, step, body):
    def trip(i, carry):
        for k in range(step):
            body(i * step + k)
        return carry

    assert count % step == 0
    lax.fori_loop(0, count // step, trip, 0)


def kernel(nx, ny, radius, terms, *refs):
    given, out, held, refs = refs[:2], refs[2], refs[3:12], refs[12:]
    taps, ry1, rz1, ry2, rz2, uy2, uz2, uy1, uz1 = held
    (fine, mid, ext, got, tips, tips_in, low1, high1, l2p, cols2, seen2, top,
           ty0, ty1, ty2, tz0, tz1, tz2, y0, s0, y1, s1, y2, s2, r1, l1w, l2y, tx, ty, md, my,
     edge, edge_in, part, send, recv, load) = refs
    bx, by, bz = given[1].shape
    x0, x1 = radius, radius + bx
    hx, hy, hz = bx // 2, by // 2, bz // 2
    ex, ey, ez = bx // 4, by // 4, bz // 4
    count = 2 * radius + 1
    margin = radius + 1
    me_x, me_y = lax.axis_index("gx"), lax.axis_index("gy")
    reach = 2
    odd = lax.rem(me_x, 2) if nx % 2 == 0 else 0
    even = 1 - odd
    wy = min(ny, 2 * reach + 1)
    low_y = -((wy - 1) // 2)

    def device(dx, dy):
        return {"gx": lax.rem(me_x + dx + nx, nx), "gy": lax.rem(me_y + dy + ny, ny)}

    peers = {}
    for dx, dy in [(-1, 0), (1, 0), (0, -1), (0, 1), (-2, 0), (2, 0)] + [
        (0, -(low_y + k)) for k in range(wy)
    ]:
        if dx % nx or dy % ny:
            peers[(dx % nx, dy % ny)] = (dx, dy)
    barrier = pltpu.get_barrier_semaphore()
    for dx, dy in peers.values():
        pl.semaphore_signal(barrier, inc=1, device_id=device(dx, dy), device_id_type=MESH)

    fetched = [
        pltpu.make_async_copy(source, target, load.at[n])
        for n, (source, target) in enumerate(zip(given, [taps, fine.at[x0:x1, 0:by]]))
    ]
    for copy in fetched:
        copy.start()

    def tap(level, member, position):
        return taps[level, member, position]

    def band(level, member, rows, cols, first, cycle, places):
        column = lax.broadcasted_iota(jnp.int32, (rows, cols), 1)
        place = column
        for start, shift in places:
            place = jnp.where(column >= start, column + shift, place)
        offsets = place - lax.broadcasted_iota(jnp.int32, (rows, cols), 0) + first
        if cycle:
            offsets = jnp.where(offsets < 0, offsets + cycle, offsets)
            offsets = jnp.where(offsets >= cycle, offsets - cycle, offsets)
        table = jnp.zeros((rows, cols), F32)
        for position in range(count):
            table = jnp.where(offsets == position, tap(level, member, position), table)
        return table

    def y_table(ref, level, rows, cols, first, cycle, places):
        for member in range(terms):
            high, low = halves(band(level, member, rows, cols, first, cycle, places))
            at = slice(member * rows, (member + 1) * rows)
            ref[at, 0:cols] = high
            ref[at, cols : 2 * cols] = high
            ref[at, 2 * cols : 3 * cols] = low

    def z_table(ref, level, n):
        def rows_of(i):
            start = pl.multiple_of(i * 16, 16)
            offsets = (
                lax.broadcasted_iota(jnp.int32, (16, n), 0)
                + start
                - lax.broadcasted_iota(jnp.int32, (16, n), 1)
                + radius
            )
            offsets = jnp.where(offsets < 0, offsets + n, offsets)
            offsets = jnp.where(offsets >= n, offsets - n, offsets)
            for member in range(terms):
                table = jnp.zeros((16, n), F32)
                for position in range(count):
                    table = jnp.where(offsets == position, tap(level, member, position), table)
                high, low = halves(table)
                ref[0, pl.ds(pl.multiple_of(member * n + start, 16), 16), :] = high
                ref[1, pl.ds(pl.multiple_of(member * n + start, 16), 16), :] = low

        repeat(n // 16, 1, rows_of)

    sem = [0]

    def remote(source, target, dx, dy):
        index = sem[0]
        sem[0] += 1
        return pltpu.make_async_remote_copy(
            src_ref=source, dst_ref=target, send_sem=send.at[index], recv_sem=recv.at[index],
            device_id=device(dx, dy), device_id_type=MESH,
        )

    def both(copies):
        for copy in copies:
            copy.start()
        return copies

    def arrive(copies):
        for copy in copies:
            copy.wait_recv()

    extra = radius - 8
    per = 8 // extra
    tip = margin - 7
    tip_per = 8 // tip
    def weighted(source, i, low, high):
        total = None
        for k in range(-2, 3):
            if low <= 2 * i + k < high:
                piece = source(2 * i + k) * SPLINE[k + 2]
                total = piece if total is None else total + piece
        return total

    def places(shape, axis):
        return lax.broadcasted_iota(jnp.int32, shape, axis)

    def spline_table(ref, offset, valid):
        distance = jnp.abs(offset)
        value = jnp.where(distance == 0, SPLINE[2], jnp.where(distance == 1, SPLINE[1], jnp.where(distance == 2, SPLINE[0], 0.0)))
        ref[...] = jnp.where(valid, value, 0.0).astype(BF16)

    def folded(index, width):
        return jnp.where(index >= width, index - width, index)

    def along_z(ref, fine_axis, n, blocks):
        rows, cols = places(ref.shape, fine_axis), places(ref.shape, 1 - fine_axis)
        same = (rows >= n) == (cols >= n // 2) if blocks == 2 else rows >= 0
        offset = folded(rows, n) - 2 * folded(cols, n // 2) if blocks == 2 else rows - 2 * cols
        offset = jnp.where(offset > n // 2, offset - n, jnp.where(offset < -(n // 2), offset + n, offset))
        spline_table(ref, offset, same)

    a, b = places(ry1.shape, 0), folded(places(ry1.shape, 1), by)
    spline_table(ry1, b - 2 * jnp.where(a == hy + 1, -1, a), a <= hy + 1)
    a, b = places(ry2.shape, 0), folded(places(ry2.shape, 1), ry1.shape[0])
    spline_table(ry2, jnp.where(b == hy + 1, -1, b) - 2 * jnp.where(a == ey + 2, -1, a), (a <= ey + 2) & (b <= hy + 1))
    a, b = places(uy2.shape, 0), folded(places(uy2.shape, 1), ry2.shape[0])
    spline_table(uy2, a + 1 - 2 * b, (a < hy + 2) & (b < ey + 3))
    a, b = places(uy1.shape, 0), folded(places(uy1.shape, 1), ry1.shape[0])
    spline_table(uy1, a + 2 - 2 * b, b < hy + 2)
    along_z(rz1, 0, bz, 1)
    along_z(uz1, 1, bz, 1)
    along_z(rz2, 0, hz, 2)
    along_z(uz2, 1, hz, 1)
    for copy in fetched:
        copy.wait()
    rows1, rows2 = hx + 2, ex + 3
    half2 = l2p.shape[0]
    wide1, wide2 = ry1.shape[0], ry2.shape[0]
    for i in range(rows1):
        r1[i] = dot(ry1[...], stacked2(weighted(lambda f: fine[x0 + f, 0:by], i - 1, 0, bx)))
    high, low = halves(r1[...].reshape(rows1 * wide1, bz))
    l1w[...] = (dot(high, rz1[...]) + dot(low, rz1[...])).reshape(rows1, wide1, hz)
    for i in range(rows2):
        l2y[i] = dot(ry2[...], stacked2(weighted(lambda f: l1w[f + 1], i - 1, -1, hx + 1)))
    for i in range(rows2, 2 * half2):
        l2y[i] = jnp.zeros((wide2, hz), F32)
    high, low = halves(jnp.concatenate([l2y[0:half2], l2y[half2 : 2 * half2]], axis=2).reshape(half2 * wide2, 2 * hz))
    l2p[...] = (dot(high, rz2[...]) + dot(low, rz2[...])).reshape(l2p.shape)
    pl.semaphore_wait(barrier, len(peers))
    lines = both([
        remote(l2p, seen2.at[0], 1, 0),
        remote(l2p, seen2.at[1], -1, 0),
        remote(l2p, seen2.at[2], 2, 0),
        remote(l2p, seen2.at[3], -2, 0),
    ])
    def edge_at(ref, d, i):
        return ref.at[d, i // 4, 2 * (i % 4) : 2 * (i % 4) + 2]

    first1 = (rows1 - margin - 1, 0)
    rim = []
    for d, dx in ((0, 1), (1, -1)):
        rim.append(remote(l1w.at[first1[d] : first1[d] + margin + 1, 0:hy], (low1, high1)[d], dx, 0))
        rim[-1].start()
    for i in range(margin + 1):
        for d in range(2):
            edge_at(edge, d, i)[...] = l1w[first1[d] + i, hy : hy + 2]
    rim += both([remote(edge.at[d], edge_in.at[d], dx, 0) for d, dx in ((0, 1), (1, -1))])
    g1 = bx // per
    steps = near_steps(radius)
    side = both([
        remote(fine.at[x0:x1, by - 8 : by], fine.at[x0:x1, by : by + 8], 0, 1),
        remote(fine.at[x0:x1, 0:8], fine.at[x0:x1, by + 8 : by + 16], 0, -1),
    ])
    for i in range(bx):
        g, r = i // per, extra * (i % per)
        ext[0, g, r : r + extra] = fine[x0 + i, by - radius : by - 8]
        ext[1, g, r : r + extra] = fine[x0 + i, 8:radius]

    side += both([
        remote(ext.at[0, 0:g1], got.at[0, 0:g1], 0, 1),
        remote(ext.at[1, 0:g1], got.at[1, 0:g1], 0, -1),
    ])
    def pick(first, second):
        return even * first + odd * second

    def span(start, size):
        return pl.ds(start, size)

    near = [
        both([remote(fine.at[span(pick(x1 - b, x0 + a), b - a), 0:by], fine.at[span(pick(x0 - b, x1 + a), b - a), 0:by], even - odd, 0)])
        for a, b in steps
    ]
    places2 = []
    for k in range(wy):
        at = wide2 * k
        places2 += [(at, ey * k - at), (at + ey + 2, ey * k - 3 - ey - at), (at + ey + 3, 1000)]
    y_table(ty2, 2, wide2, wy * wide2, low_y * ey + 1 + radius, wy * ey if ny <= 2 * reach + 1 else 0, places2)
    z_table(tz2, 2, ez)
    y_table(ty0, 0, by, by + 24, radius, 0, [(by, -by - 8), (by + 8, -8), (by + 16, -by - 16 - radius), (by + 16 + extra, -8 - extra), (by + 16 + 2 * extra, 1000)])
    low, high = wide1 + 16, wide1 + 16 + tip
    y_table(ty1, 1, wide1, wide1 + 16 + 2 * tip, radius + 1, 0, [
        (hy + 1, -hy - 2), (hy + 2, 1000), (wide1, -8 - wide1), (wide1 + 8, hy - wide1 - 8), (low, -margin - low),
        (low + tip - 1, -low - tip + 1), (high, hy + 8 - high), (high + tip - 1, hy - high - tip),
    ])
    z_table(tz0, 0, bz)
    spare = jnp.zeros((8 - 2 * extra, bz), F32)

    def unpack(rows, first):
        for n, i in enumerate(rows):
            g, r = first + n // per, extra * (n % per)
            fine[i, by + 16 : by + 16 + extra] = got[0, g, r : r + extra]
            fine[i, by + 16 + extra : by + 16 + 2 * extra] = got[1, g, r : r + extra]
            fine[i, by + 16 + 2 * extra : by + 24] = spare

    z_table(tz1, 1, hz)

    arrive(lines)
    home = radius
    pairs = cols2.shape[1]
    whole = [None] * (2 * pairs)
    for first, source in ((home, l2p), (home - ex, seen2.at[0]), (home + ex, seen2.at[1]), (home - 2 * ex, seen2.at[2]), (home + 2 * ex, seen2.at[3])):
        for r in range(rows2):
            if 0 <= first + r < rows2 + 2 * radius:
                piece = source[r % half2][:, (r // half2) * ez : (r // half2 + 1) * ez]
                whole[first + r] = piece if whole[first + r] is None else whole[first + r] + piece
    for j in range(pairs):
        top[j] = jnp.concatenate([jnp.zeros((wide2, ez), F32) if v is None else v for v in (whole[j], whole[j + pairs])], axis=1)
    if ny == 4:
        turn = 1 - 2 * lax.rem(me_y, 2)
        fan = both([remote(top, cols2.at[3], 0, 2), remote(top, cols2.at[1 - turn], 0, turn)])
    else:
        fan = both([remote(top, cols2.at[k], 0, -(low_y + k)) for k in range(wy) if low_y + k])
    cols2[-low_y] = top[...]
    def correlate_y(ref, source, table, rows, step, first=0):
        width = table.shape[0] // terms

        def one(i):
            i = i + first
            value = dot(table[...], stacked3(source[i]))
            for member in range(terms):
                ref[member, i] = value[member * width : (member + 1) * width]

        repeat(rows, step, one)

    def correlate_x(ref, source, level, rows, first, step, start=0):
        def one(i):
            i = i + start
            for member in range(terms):
                total = None
                for position in range(count):
                    piece = source[member, i + first + position] * tap(level, member, position)
                    total = piece if total is None else total + piece
                high, low = halves(total)
                at = slice(member * total.shape[1], (member + 1) * total.shape[1])
                ref[0, i, :, at] = high
                ref[1, i, :, at] = low

        repeat(rows, step, one)

    mid[:, hy:wide1] = jnp.zeros((mid.shape[0], wide1 - hy, hz), F32)
    mid[margin + 1 : margin + hx - 1, 0:wide1] = l1w[2:hx]
    arrive(rim)
    mid[0 : margin + 1, 0:hy] = low1[...]
    mid[margin + hx - 1 : margin + hx + margin, 0:hy] = high1[...]
    for i in range(margin + 1):
        for d, at in ((0, 0), (1, margin + hx - 1)):
            mid[at + i, hy : hy + 2] = edge_at(edge_in, d, i)[...]
    for i, j in ((margin - 1, 0), (margin, 1), (margin + hx - 1, hx), (margin + hx, hx + 1)):
        mid[i, 0:wide1] += l1w[j]
    rim2 = both([
        remote(mid.at[:, hy - 8 : hy], mid.at[:, wide1 : wide1 + 8], 0, 1),
        remote(mid.at[:, 0:8], mid.at[:, wide1 + 8 : wide1 + 16], 0, -1),
    ])
    for i in range(mid.shape[0]):
        g, r = i // tip_per, tip * (i % tip_per)
        for d, (a, b) in enumerate(((hy - margin, hy - 8), (8, margin))):
            tips[d, g, r : r + tip - 1] = mid[i, a:b]
            tips[d, g, r + tip - 1 : r + tip] = mid[i, hy + d : hy + d + 1]
    rim2 += both([remote(tips.at[d], tips_in.at[d], 0, dy) for d, dy in ((0, 1), (1, -1))])
    far = [
        both([remote(fine.at[span(pick(x0 + a, x1 - b), b - a), 0:by], fine.at[span(pick(x1 + a, x0 - b), b - a), 0:by], odd - even, 0)])
        for a, b in steps
    ]

    def correlate_z(ref, table, rows, count):
        size = count * ref.shape[2]
        high = ref[0, rows].reshape(size, ref.shape[3])
        low = ref[1, rows].reshape(size, ref.shape[3])
        return dot(high, table[0]) + dot(low, table[0]) + dot(high, table[1])

    def prolong_x(source, j, first):
        at = j - 2 * first
        if j % 2 == 0:
            c = (j // 2) - first
            return source[c - 1] * 0.125 + source[c] * 0.75 + source[c + 1] * 0.125
        c = (j - 1) // 2 - first
        return source[c] * 0.5 + source[c + 1] * 0.5

    arrive(side)
    unpack(range(x0, x1), 0)
    correlate_y(y0, fine, ty0, bx, 4, x0)
    correlate_x(s0, y0, 0, bx - 2 * radius, 0, 1, radius)
    if ny == 4:
        arrive(fan[:1])
        fan = both([remote(cols2.at[3], cols2.at[1 + turn], 0, turn)]) + fan[1:] + fan[:1]
    for e in range(radius):
        for edge_of, i in ((0, e), (1, bx - 1 - e)):
            for member in range(terms):
                total = None
                for position in range(count):
                    if x0 <= i + position < x1:
                        piece = y0[member, i + position] * tap(0, member, position)
                        total = piece if total is None else total + piece
                part[edge_of, e, member] = total

    def add_halo(edge_of, a, b):
        def choose(first, last):
            return (1 - edge_of) * first + edge_of * last

        for e in range(radius - a):
            i = choose(e, bx - 1 - e)
            for member in range(terms):
                total = part[edge_of, e, member]
                for k in range(a, min(b, radius - e)):
                    weight = tap(0, member, choose(radius - 1 - k - e, radius + 1 + k + e))
                    total = total + y0[member, choose(x0 - 1 - k, x1 + k)] * weight
                if radius - e > b:
                    part[edge_of, e, member] = total
                else:
                    high, low = halves(total)
                    s0[0, i, :, member * bz : (member + 1) * bz] = high
                    s0[1, i, :, member * bz : (member + 1) * bz] = low

    def pack(start, size, group):
        for n in range(size):
            g, r = group + n // per, extra * (n % per)
            ext[0, g, r : r + extra] = fine[start + n, by - radius : by - 8, :]
            ext[1, g, r : r + extra] = fine[start + n, 8:radius, :]
        rows, groups = span(start, size), slice(group, group - (-size // per))
        return both([
            remote(fine.at[rows, by - 8 : by], fine.at[rows, by : by + 8], 0, 1),
            remote(fine.at[rows, 0:8], fine.at[rows, by + 8 : by + 16], 0, -1),
            remote(ext.at[0, groups], got.at[0, groups], 0, 1),
            remote(ext.at[1, groups], got.at[1, groups], 0, -1),
        ])

    parts = [(a, b, pick(x0 - b, x1 + a), pick(radius - b, bx - radius + a), odd) for a, b in steps] + [
        (a, b, pick(x1 + a, x0 - b), pick(bx - radius + a, radius - b), even) for a, b in steps
    ]
    groups = [g1]
    for a, b, _, _, _ in parts:
        groups.append(groups[-1] + -(-(b - a) // per))
    corners = []

    def relay(copies):
        n = len(corners)
        a, b, halo, _, _ = parts[n]
        arrive(copies)
        corners.append(pack(halo, b - a, groups[n]))

    arrive(fan[:2] if ny == 4 else fan)
    for j in range(pairs):
        value = dot(ty2[...], stacked3(jnp.concatenate([cols2[k, j] for k in range(wy)], axis=0)))
        for member in range(terms):
            y2[member, j] = value[member * wide2 : (member + 1) * wide2, 0:ez]
            y2[member, j + pairs] = value[member * wide2 : (member + 1) * wide2, ez : 2 * ez]
    correlate_x(s2, y2, 2, rows2, 0, rows2)
    tx[...] = correlate_z(s2, tz2, slice(0, rows2), rows2).reshape(tx.shape)
    for j in range(hx + 2):
        ty[j] = dot(uy2[...], stacked2(prolong_x(tx, j - 1, -1)))
    high, low = halves(ty[...].reshape((hx + 2) * ty.shape[1], ez))
    lifted = dot(high, uz2[...]) + dot(low, uz2[...])

    md[...] = lifted.reshape(md.shape)
    relay(far[0])
    arrive(rim2)
    for i in range(mid.shape[0]):
        g, r = i // tip_per, tip * (i % tip_per)
        for d in range(2):
            mid[i, wide1 + 16 + tip * d : wide1 + 16 + tip * (d + 1)] = tips_in[d, g, r : r + tip]
    correlate_y(y1, mid, ty1, hx + 2 * margin, (hx + 2 * margin) // 2)
    early = (hx + 2) // 2
    correlate_x(s1, y1, 1, early, 0, early)
    relay(far[1])
    correlate_x(s1, y1, 1, hx + 2 - early, 0, hx + 2 - early, early)
    md[...] += correlate_z(s1, tz1, slice(0, hx + 2), hx + 2).reshape(md.shape)
    for j in range(0, bx, 2):
        pair = jnp.concatenate([prolong_x(md, j, -1), prolong_x(md, j + 1, -1)], axis=1)
        high, low = halves(dot(uy1[...], stacked2(pair)))
        for k in range(2):
            my[0, j + k] = high[:, k * hz : (k + 1) * hz]
            my[1, j + k] = low[:, k * hz : (k + 1) * hz]

    def finish(start, size):
        rows = span(start, size)
        high = my[0, rows].reshape(size * by, hz)
        low = my[1, rows].reshape(size * by, hz)
        total = correlate_z(s0, tz0, rows, size) + dot(high, uz1[...]) + dot(low, uz1[...])
        out[rows] = total.reshape(size, by, bz)

    relay(near[0])
    finish(radius, bx - 2 * radius)
    for n, (a, b, halo, target, edge_of) in enumerate(parts):
        arrive(corners[n])
        unpack([halo + k for k in range(b - a)], groups[n])
        correlate_y(y0, fine, ty0, b - a, (b - a) // 2, halo)
        add_halo(edge_of, a, b)
        if n == 0:
            relay(near[1])
        finish(target, b - a)
    for copy in fan + rim + side + lines + sum(near + far, []) + rim2 + sum(corners, []):
        copy.wait_send()


def near_steps(radius):
    first = min(radius, radius // 2 + radius // 2 % 2)
    return [(0, first), (first, radius)]


def body(charges, kernel_taps):
    nx, ny = lax.axis_size("gx"), lax.axis_size("gy")
    levels, terms, count = kernel_taps.shape
    radius = count // 2
    margin = radius + 1
    bx, by, bz = charges.shape
    hx, hy, hz = bx // 2, by // 2, bz // 2
    ex, ey, ez = bx // 4, by // 4, bz // 4
    wy = min(ny, 5)
    wide1 = hy + 8
    wide2 = ey + 8
    tables = [(wide1, 2 * by), (bz, hz), (wide2, 2 * wide1), (2 * hz, 2 * ez), (wide1, 2 * wide2), (ez, hz), (by, 2 * wide1), (hz, bz)]
    rows1, rows2 = hx + 2, ex + 3
    half2, pairs = (rows2 + 1) // 2, (rows2 + 2 * radius + 1) // 2
    extra = radius - 8
    tip = margin - 7
    packed = bx * extra // 8 + sum(-(-(b - a) * extra // 8) for a, b in 2 * near_steps(radius))
    scratch = [pltpu.SMEM(kernel_taps.shape, F32)] + [pltpu.VMEM(shape, BF16) for shape in tables] + [
        pltpu.VMEM(shape, dtype)
        for shape, dtype in (
            ((bx + 2 * radius, by + 24, bz), F32),
            ((hx + 2 * margin, wide1 + 16 + 2 * tip, hz), F32),
            ((2, packed, 8, bz), F32),
            ((2, packed, 8, bz), F32),
            ((2, -(-(hx + 2 * margin) // (8 // tip)), 8, hz), F32),
            ((2, -(-(hx + 2 * margin) // (8 // tip)), 8, hz), F32),
            ((margin + 1, hy, hz), F32),
            ((margin + 1, hy, hz), F32),
            ((half2, wide2, 2 * ez), F32),
            ((wy, pairs, wide2, 2 * ez), F32),
            ((4, half2, wide2, 2 * ez), F32),
            ((pairs, wide2, 2 * ez), F32),
            ((terms * by, 3 * (by + 24)), BF16),
            ((terms * wide1, 3 * (wide1 + 16 + 2 * tip)), BF16),
            ((terms * wide2, 3 * wy * wide2), BF16),
            ((2, terms * bz, bz), BF16),
            ((2, terms * hz, hz), BF16),
            ((2, terms * ez, ez), BF16),
            ((terms, bx + 2 * radius, by, bz), F32),
            ((2, bx, by, terms * bz), BF16),
            ((terms, hx + 2 * margin, wide1, hz), F32),
            ((2, hx + 2, wide1, terms * hz), BF16),
            ((terms, 2 * pairs, wide2, ez), F32),
            ((2, rows2, wide2, terms * ez), BF16),
            ((rows1, wide1, bz), F32),
            ((rows1, wide1, hz), F32),
            ((2 * half2, wide2, hz), F32),
            ((rows2, wide2, ez), F32),
            ((hx + 2, wide1, ez), F32),
            ((hx + 2, wide1, hz), F32),
            ((2, bx, by, hz), BF16),
            ((2, -(-2 * (margin + 1) // 8), 8, hz), F32),
            ((2, -(-2 * (margin + 1) // 8), 8, hz), F32),
            ((2, radius, terms, by, bz), F32),
        )
    ] + [
        pltpu.SemaphoreType.DMA((40,)),
        pltpu.SemaphoreType.DMA((40,)),
        pltpu.SemaphoreType.DMA((2,)),
    ]
    result = pl.pallas_call(
        functools.partial(kernel, nx, ny, radius, terms),
        out_shape=jax.ShapeDtypeStruct(charges.shape, F32),
        in_specs=[pl.BlockSpec(memory_space=pltpu.HBM)] * 2,
        out_specs=pl.BlockSpec(memory_space=pltpu.VMEM),
        scratch_shapes=scratch,
        compiler_params=pltpu.CompilerParams(
            collective_id=0, has_side_effects=True, vmem_limit_bytes=211 * 2**18
        ),
    )(kernel_taps, charges)
    return result


def solution(mesh):
    return jax.shard_map(
        body,
        mesh=mesh,
        in_specs=(P("gx", "gy", None), P()),
        out_specs=P("gx", "gy", None),
        check_vma=False,
    )
```
